32 devices in a mesh: fsdp: 8 (over z, x), ctx: 4 (over y, core).
Axes of the slice: x: 2, y: 2, z: 4, core: 2. Of those that a mesh axis runs over, the one named last changes fastest.
Arguments:
- tokens: bfloat16 [16, 592, 1024], P('fsdp', 'ctx'), may hold values from -6 to 6
- out_grad: bfloat16 [16, 592, 1024], P('fsdp', 'ctx'), may hold values from -6 to 6
- key_mask: int32 [16, 592], P('fsdp', 'ctx'), may hold values from 0 to 1, as said below
- slot_valid: int32 [16], P('fsdp'), may hold values 0 or 1
- norm_gains: bfloat16 [2, 1024], P(None, 'fsdp'), may hold values from 0.25 to 1.75
- norm_shifts: bfloat16 [2, 1024], P(None, 'fsdp'), may hold values from -2 to 2
- qkv_weight: bfloat16 [1024, 3072], P('fsdp'), may hold values from -0.1875 to 0.1875
- qv_bias: bfloat16 [2, 1024], P(None, 'fsdp'), may hold values from -3 to 3
- out_weight: bfloat16 [1024, 1024], P('fsdp'), may hold values from -1.5 to 1.5
- out_bias: bfloat16 [1024], P('fsdp'), may hold values from -2 to 2
- fc1_weight: bfloat16 [1024, 4096], P('fsdp'), may hold values from -0.1875 to 0.1875
- fc1_bias: bfloat16 [4096], P('fsdp'), may hold values from -3 to 3
- fc2_weight: bfloat16 [4096, 1024], P('fsdp'), may hold values from -0.125 to 0.125
- fc2_bias: bfloat16 [1024], P('fsdp'), may hold values from -2 to 2
Outputs:
- result: bfloat16 [16, 592, 1024], P('fsdp', 'ctx')
- token_gradient: bfloat16 [16, 592, 1024], P('fsdp', 'ctx')
- gain_grads: float32 [2, 1024], P(None, 'fsdp')
- shift_grads: float32 [2, 1024], P(None, 'fsdp')
- qkv_grad: float32 [1024, 3072], P('fsdp')
- qv_bias_grad: float32 [2, 1024], P(None, 'fsdp')
- out_weight_grad: float32 [1024, 1024], P('fsdp')
- out_bias_grad: float32 [1024], P('fsdp')
- fc1_grad: float32 [1024, 4096], P('fsdp')
- fc1_bias_grad: float32 [4096], P('fsdp')
- fc2_grad: float32 [4096, 1024], P('fsdp')
- fc2_bias_grad: float32 [1024], P('fsdp')
The draws below stay inside these ranges and needn't reach their ends.
Inputs may be any that keep to these rules, and one draw needn't show every extreme that they name: key_mask is 1 at position 0 of every image and 0 at positions 577 and beyond.
All inputs are finite; a program needn't handle non-finite values. No bound on the sum of `slot_valid` on one device may be relied on, other than what follows from the above.
Results may differ from the reference program's by a relative error of at most 0.017.
Values may be sent and summed in bfloat16 or wider, within the bound.
No kernel may reach another device: no remote copies, remote signals or barrier semaphores. Data moves between devices by JAX's collectives and lax.ppermute only.
A program may use at most 192 MiB of HBM per device.

```python
import jax
import jax.numpy as jnp
from jax import lax

D = 1024
HEADS = 16
HEAD_DIM = 64
FF = 4096
SEQ = 592
LIVE = 577
IMG_DEV = 2
IMAGES = 16
N_FSDP = 8


def draw_key_mask(key, part):
    position = jnp.arange(SEQ)[None, :]
    kept = jax.random.randint(key, (IMAGES, SEQ), 0, 4) > 0
    live = (position < LIVE) & (kept | (position == 0))
    return live.astype(jnp.int32)


def with_ends(entries, stream_key, least, top_value):
    longest = entries.shape.index(max(entries.shape))
    spots = []
    for shift in (0, 1):
        where = [jax.random.randint(jax.random.fold_in(stream_key, axis), (), 0, length) for axis, length in enumerate(entries.shape)]
        where[longest] = (where[longest] + shift) % entries.shape[longest]
        spots.append(tuple(where))
    return entries.at[spots[0]].set(least).at[spots[1]].set(top_value)


def with_spikes(array, stream_key, source, target, parts, factor):
    def block_of(axis_at):
        return (jnp.arange(array.shape[axis_at]) // (array.shape[axis_at] // parts)).reshape((-1,) + (1,) * (array.ndim - 1 - axis_at))

    first = jax.random.permutation(stream_key, parts)[block_of(target)]
    far = (block_of(target) + parts // 2) % parts
    return jnp.where((block_of(source) == first) | (block_of(source) == far), factor * array, array)


def block_levels(own_key, extent, pieces, least, high):
    level, own = 1.0, jax.random.fold_in(own_key, 6)
    for dim, shards_of in pieces:
        steps = jnp.exp(jax.random.uniform(jax.random.fold_in(own, dim), (shards_of,), jnp.float32, least / len(pieces), high / len(pieces)))
        level = level * jnp.repeat(steps, extent[dim] // shards_of).reshape([-1 if axis == dim else 1 for axis in range(len(extent))])
    return level


def bell_draw(rng, dims, scale, reach, pieces=(), dtype=jnp.bfloat16):
    values = scale * jax.random.normal(rng, dims, jnp.float32)
    if pieces:
        values = values * block_levels(rng, dims, pieces, -0.22, 0.18)
    return jnp.clip(values, -reach, reach).astype(dtype)


def bell_draw_with(key, shape, width, reach, pieces, heavy, kind=jnp.bfloat16):
    array = width * jax.random.normal(key, shape, jnp.float32)
    if pieces:
        array = array * block_levels(key, shape, pieces, -0.22, 0.18)
    return jnp.clip(with_spikes(array, jax.random.fold_in(key, 3), *heavy), -reach, reach).astype(kind)


def setup_inputs(seed: int = 0) -> dict:
    keys = jax.random.split(jax.random.key(seed), 15)
    return {
        "tokens": bell_draw(keys[0], (IMAGES, SEQ, D), 1.0, 6.0, ((0, 8), (1, 4))),
        "out_grad": bell_draw_with(keys[1], (IMAGES, SEQ, D), 1.0, 6.0, ((0, 8), (1, 4)), (0, 2, 8, 2.0)),
        "key_mask": draw_key_mask(jax.random.fold_in(keys[14], 71), 0),
        "slot_valid": with_ends((jax.random.randint(keys[3], (IMAGES,), 0, 8) < 7).astype(jnp.int32), jax.random.fold_in(keys[3], 1), 0, 1),
        "norm_gains": jnp.clip(1.0 + 0.15 * jax.random.normal(keys[4], (2, D), jnp.float32), 0.25, 1.75).astype(jnp.bfloat16),
        "norm_shifts": bell_draw(keys[5], (2, D), 0.3, 2.0, ((1, 8),)),
        "qkv_weight": bell_draw(keys[6], (D, 3 * D), D ** -0.5, 0.1875, ((0, 8),)),
        "qv_bias": bell_draw(keys[7], (2, D), 0.5, 3.0, ((1, 8),)),
        "out_weight": bell_draw(keys[8], (D, D), (max(D // 64, 1)) ** -0.5, 1.5, ((0, 8),)),
        "out_bias": bell_draw(keys[9], (D,), 0.3, 2.0, ((0, 8),)),
        "fc1_weight": bell_draw(keys[10], (D, FF), D ** -0.5, 0.1875, ((0, 8),)),
        "fc1_bias": bell_draw(keys[11], (FF,), 0.5, 3.0, ((0, 8),)),
        "fc2_weight": bell_draw(keys[12], (FF, D), (FF // 2) ** -0.5, 0.125, ((0, 8),)),
        "fc2_bias": bell_draw(keys[13], (D,), 0.3, 2.0, ((0, 8),)),
    }


@jax.custom_vjp
def low(v):
    return lax.optimization_barrier(v.astype(jnp.bfloat16)).astype(jnp.float32)

@jax.custom_vjp
def low_back(v):
    return v

def low_keep(v):
    return (low(v), None)

def low_pass(kept, grad):
    return (grad,)

def back_keep(v):
    return (v, None)

def back_low(kept, grad):
    return (low(grad),)
low.defvjp(low_keep, low_pass)
low_back.defvjp(back_keep, back_low)

def apply_layer_norm(values, gain_row, shift_row):
    centred = values - lax.optimization_barrier(jnp.mean(values, axis=-1, keepdims=True))
    inverse_std = lax.rsqrt(lax.optimization_barrier(jnp.mean(centred * centred, axis=-1, keepdims=True)) + 1e-05)
    return centred * inverse_std * gain_row + shift_row

def product(left_side, right_side):
    return jnp.dot(left_side, right_side, precision=lax.Precision.HIGHEST)

def forward(params, inputs, visible):
    norm_gain_vector, norm_bias_vector, qkv_matrix, qv_shift, out_matrix, out_shift, fc1_matrix, fc1_shift, fc2_matrix, fc2_shift = params
    flattened_rows = inputs.reshape(IMG_DEV * SEQ, D)
    normed = low(apply_layer_norm(flattened_rows, norm_gain_vector[0], norm_bias_vector[0]))
    raw_proj = low_back(product(normed, qkv_matrix))
    head_shape = (IMG_DEV, SEQ, HEADS, HEAD_DIM)
    queries = low(raw_proj[:, :D] + qv_shift[0]).reshape(head_shape)
    key_heads = low(raw_proj[:, D:2 * D]).reshape(head_shape)
    value_heads = low(raw_proj[:, 2 * D:] + qv_shift[1]).reshape(head_shape)
    scores = low_back(jnp.einsum('bqhd,bkhd->bhqk', queries, key_heads, precision=lax.Precision.HIGHEST) * 0.125)
    scores = jnp.where(visible[:, None, None, :], scores, -1e+30)
    row_max = lax.optimization_barrier(jnp.max(scores, axis=-1, keepdims=True))
    exponent = jnp.exp(scores - row_max)
    attention_weights = low(exponent / lax.optimization_barrier(jnp.sum(exponent, axis=-1, keepdims=True)))
    context = jnp.einsum('bhqk,bkhd->bqhd', attention_weights, value_heads, precision=lax.Precision.HIGHEST)
    context = low_back(low(context.reshape(IMG_DEV * SEQ, D)))
    residual_state = flattened_rows + low_back(product(context, out_matrix)) + out_shift
    normalized_residual = low(apply_layer_norm(residual_state, norm_gain_vector[1], norm_bias_vector[1]))
    pre_act = low_back(product(normalized_residual, fc1_matrix)) + fc1_shift
    hidden = low(pre_act * jax.nn.sigmoid(1.702 * pre_act))
    output = residual_state + product(hidden, fc2_matrix) + fc2_shift
    return output.reshape(IMG_DEV, SEQ, D)

def add_up(first, second):
    return first + second

def reference(tokens, out_grad, key_mask, slot_valid, norm_gains, norm_shifts, qkv_weight, qv_bias, out_weight, out_bias, fc1_weight, fc1_bias, fc2_weight, fc2_bias):
    params = (norm_gains.astype(jnp.float32), norm_shifts.astype(jnp.float32), qkv_weight.astype(jnp.float32), qv_bias.astype(jnp.float32), out_weight.astype(jnp.float32), out_bias.astype(jnp.float32), fc1_weight.astype(jnp.float32), fc1_bias.astype(jnp.float32), fc2_weight.astype(jnp.float32), fc2_bias.astype(jnp.float32))
    position = jnp.arange(SEQ)
    row_keep = (position < LIVE)[None, :] & (slot_valid[:, None] > 0)
    cotangent = jnp.where(row_keep[:, :, None], out_grad.astype(jnp.float32), jnp.zeros((), jnp.float32))
    inputs_all = tokens.astype(jnp.float32).reshape(N_FSDP, IMG_DEV, SEQ, D)
    cotangent_all = cotangent.reshape(N_FSDP, IMG_DEV, SEQ, D)
    visible_all = (key_mask > 0).reshape(N_FSDP, IMG_DEV, SEQ)

    def image_step(summed, group_item):
        inputs, grad_here, visible = group_item

        def layer_fn(layer_params, layer_inputs):
            return forward(layer_params, layer_inputs, visible)
        output, pullback = jax.vjp(layer_fn, params, inputs)
        grad_params, grad_inputs = pullback(grad_here)
        summed = jax.tree.map(add_up, summed, grad_params)
        return (summed, (output.astype(jnp.bfloat16), grad_inputs.astype(jnp.bfloat16)))
    zero_grads = jax.tree.map(jnp.zeros_like, params)
    summed, outputs = lax.scan(image_step, zero_grads, (inputs_all, cotangent_all, visible_all))
    result = outputs[0].reshape(IMAGES, SEQ, D)
    token_gradient = outputs[1].reshape(IMAGES, SEQ, D)
    return (result, token_gradient, summed[0], summed[1], summed[2], summed[3], summed[4], summed[5], summed[6], summed[7], summed[8], summed[9])
```

```python
import functools

import jax
import jax.numpy as jnp
from jax import lax
from jax.experimental import pallas as pl
from jax.experimental.pallas import tpu as pltpu
from jax.sharding import PartitionSpec as P

D = 1024
HEADS = 16
HEAD_DIM = 64
LIVE = 577
PAD = 160
MASK_ROW = 148
NEG = -1e30
F32 = jnp.float32
BF16 = jnp.bfloat16


def dot(a, b):
    return lax.dot_general(a, b, (((1,), (0,)), ((), ())), preferred_element_type=F32)


def dot_nt(a, b):
    return lax.dot_general(a, b, (((1,), (1,)), ((), ())), preferred_element_type=F32)


def dot_tn(a, b):
    return lax.dot_general(a, b, (((0,), (0,)), ((), ())), preferred_element_type=F32)


def layer_norm(values):
    centred = values - jnp.mean(values, axis=-1, keepdims=True)
    inverse = lax.rsqrt(jnp.mean(centred * centred, axis=-1, keepdims=True) + 1e-05)
    return centred * inverse, inverse


def norm_reverse(grad, normed, inverse):
    first = jnp.mean(grad, axis=-1, keepdims=True)
    second = jnp.mean(grad * normed, axis=-1, keepdims=True)
    return inverse * (grad - first - normed * second)


def attn_fwd_kernel(q_ref, k_ref, v_ref, bias_ref, o_ref):
    rows = q_ref.shape[0]
    lane = lax.broadcasted_iota(jnp.int32, (1, 128), 1)
    k = k_ref[...]
    v = v_ref[...]
    bias = bias_ref[...]
    for start in range(0, rows, 128):
        q = q_ref[start : start + 128, :] * 0.125
        outs = []
        for h in range(2):
            qh = jnp.where((lane // 64) == h, q, jnp.zeros_like(q))
            s = dot_nt(qh, k) + bias
            top = jnp.max(s, axis=-1, keepdims=True)
            e = jnp.exp(s - top)
            total = jnp.sum(e, axis=-1, keepdims=True)
            p = (e * (1.0 / total)).astype(BF16)
            outs.append(dot(p, v))
        o_ref[start : start + 128, :] = jnp.where(lane < 64, outs[0], outs[1]).astype(BF16)


def attn_bwd_kernel(q_ref, k_ref, v_ref, g_ref, bias_ref, dq_ref, dk_ref, dv_ref, sum_ref, dk_acc, dv_acc):
    rows = q_ref.shape[0]
    lane = lax.broadcasted_iota(jnp.int32, (1, 128), 1)
    k = k_ref[...]
    v = v_ref[...]
    bias = bias_ref[:, 0:1]
    qsum = jnp.zeros((1, 128), F32)
    for start in range(0, rows, 128):
        q = q_ref[start : start + 128, :] * 0.125
        g = g_ref[start : start + 128, :]
        dqs, dks, dvs = [], [], []
        for h in range(2):
            mine = (lane // 64) == h
            qh = jnp.where(mine, q, jnp.zeros_like(q))
            gh = jnp.where(mine, g, jnp.zeros_like(g))
            s = dot_nt(k, qh) + bias
            top = jnp.max(s, axis=0, keepdims=True)
            e = jnp.exp(s - top)
            total = jnp.sum(e, axis=0, keepdims=True)
            p = e * (1.0 / total)
            dp = dot_nt(v, gh)
            delta = jnp.sum(p * dp, axis=0, keepdims=True)
            ds = (p * (dp - delta)).astype(BF16)
            dvs.append(dot(p.astype(BF16), gh))
            dks.append(dot(ds, qh))
            dqs.append(dot_tn(ds, k))
        dq = jnp.where(lane < 64, dqs[0], dqs[1]) * 0.125
        qsum = qsum + jnp.sum(dq, axis=0, keepdims=True)
        dq_ref[start : start + 128, :] = dq.astype(BF16)
        dk = dks[0] + dks[1]
        dv = dvs[0] + dvs[1]
        if start == 0:
            dk_acc[...] = dk
            dv_acc[...] = dv
        else:
            dk_acc[...] += dk
            dv_acc[...] += dv
    dk_ref[...] = dk_acc[...].astype(BF16)
    dv = dv_acc[...]
    dv_ref[...] = dv.astype(BF16)
    vsum = jnp.sum(dv, axis=0, keepdims=True)
    sum_ref[...] = jnp.concatenate([qsum, vsum, jnp.zeros((6, 128), F32)], axis=0)


def attention(qkv, bias_row):
    rows, width = qkv.shape[0], qkv.shape[1] // 3
    pairs = width // 128
    spec = lambda off: pl.BlockSpec((rows, 128), lambda i: (0, off * pairs + i))
    return pl.pallas_call(
        attn_fwd_kernel,
        grid=(pairs,),
        in_specs=[spec(0), spec(1), spec(2), pl.BlockSpec((1, rows), lambda i: (0, 0))],
        out_specs=pl.BlockSpec((rows, 128), lambda i: (0, i)),
        out_shape=jax.ShapeDtypeStruct((rows, width), BF16),
        compiler_params=pltpu.CompilerParams(vmem_limit_bytes=40 << 20),
        cost_estimate=pl.CostEstimate(
            flops=4 * rows * rows * width * 4,
            bytes_accessed=4 * rows * width * 2,
            transcendentals=rows * rows * pairs * 2,
        ),
        name="attn_fwd",
    )(qkv, qkv, qkv, bias_row)


def attention_back(qkv, grad, bias_col):
    rows, width = grad.shape
    pairs = width // 128
    spec = lambda off: pl.BlockSpec((rows, 128), lambda i: (0, off * pairs + i))
    out = pl.BlockSpec((rows, 128), lambda i: (0, i))
    return pl.pallas_call(
        attn_bwd_kernel,
        grid=(pairs,),
        in_specs=[
            spec(0),
            spec(1),
            spec(2),
            pl.BlockSpec((rows, 128), lambda i: (0, i)),
            pl.BlockSpec((rows, 128), lambda i: (0, 0)),
        ],
        out_specs=[out, out, out, pl.BlockSpec((8, 128), lambda i: (0, i))],
        out_shape=[jax.ShapeDtypeStruct((rows, width), BF16)] * 3
        + [jax.ShapeDtypeStruct((8, width), F32)],
        scratch_shapes=[pltpu.VMEM((rows, 128), F32)] * 2,
        compiler_params=pltpu.CompilerParams(vmem_limit_bytes=48 << 20),
        cost_estimate=pl.CostEstimate(
            flops=10 * rows * rows * width * 4,
            bytes_accessed=8 * rows * width * 2,
            transcendentals=rows * rows * pairs * 2,
        ),
        name="attn_bwd",
    )(qkv, qkv, qkv, grad, bias_col)


def body(
    nf,
    nc,
    tokens,
    out_grad,
    key_mask,
    slot_valid,
    norm_gains,
    norm_shifts,
    qkv_weight,
    qv_bias,
    out_weight,
    out_bias,
    fc1_weight,
    fc1_bias,
    fc2_weight,
    fc2_bias,
):
    f = lax.axis_index("fsdp")
    c = lax.axis_index("ctx")
    axes = ("fsdp", "ctx")
    bits = []
    while (1 << len(bits)) < nf:
        bits.append(1 << len(bits))

    def swap(v, df, dc):
        pairs = [(i * nc + j, (i ^ df) * nc + (j ^ dc)) for i in range(nf) for j in range(nc)]
        return lax.ppermute(v, axes, pairs)

    def core(v):
        return swap(v, 0, 1)

    def across(v):
        return swap(v, 0, 2)

    def gather(shard, axis=0):
        buf = shard[None]
        for b in reversed(bits):
            other = swap(buf, b, 0)
            up = (f // b) % 2 == 1
            low, high = jnp.where(up, other, buf), jnp.where(up, buf, other)
            buf = jnp.stack([low, high], axis=1).reshape((2 * buf.shape[0],) + shard.shape)
        if axis == 0:
            return buf.reshape((-1,) + shard.shape[1:])
        return buf.transpose(1, 0, 2).reshape(shard.shape[0], -1)

    def scatter(full, low):
        for b in bits:
            v = full.reshape((full.shape[0] // 2, 2) + full.shape[1:])
            up = (f // b) % 2
            send = lax.dynamic_index_in_dim(v, 1 - up, 1, keepdims=False).astype(low)
            keep = lax.dynamic_index_in_dim(v, up, 1, keepdims=False)
            full = keep + swap(send, b, 0).astype(F32)
        return full[0]

    def ctx_all(v):
        other = across(v)
        up = c // 2 == 1
        v = jnp.stack([jnp.where(up, other, v), jnp.where(up, v, other)])
        other = core(v)
        up = c % 2 == 1
        v = jnp.stack([jnp.where(up, other, v), jnp.where(up, v, other)], axis=1)
        return v.reshape((4,) + v.shape[2:])

    n_img, length = tokens.shape[0], tokens.shape[1]
    quarter = D // nc
    wide = 4 * D // nf // nc

    def spread(v):
        v = jnp.concatenate([v, across(v)], axis=0)
        return jnp.concatenate([v, core(v)], axis=0)

    def all_rows(part):
        half = 2 * PAD
        mine = part[:half] + core(part[half:].astype(BF16)).astype(F32)
        got = across(mine.astype(BF16)).astype(F32)
        mine = mine + jnp.concatenate([got[PAD:], got[:PAD]], axis=0)
        rest = core(mine.astype(BF16)).astype(F32)
        return jnp.concatenate([mine, rest], axis=0)

    def own_rows(part):
        half = 2 * PAD
        mine = part[:half] + core(part[half:].astype(BF16)).astype(F32)
        return mine[:PAD] + across(mine[PAD:].astype(BF16)).astype(F32)

    x_all = []
    for i in range(n_img):
        mask_row = jnp.pad(key_mask[i : i + 1].astype(BF16), ((0, 0), (0, D - length)))
        x = jnp.concatenate(
            [tokens[i], mask_row, jnp.zeros((PAD - length - 1, D), BF16)], axis=0
        )
        x_all.append(spread(x))

    small = jnp.concatenate(
        [
            norm_gains,
            norm_shifts,
            qv_bias,
            out_bias[None],
            fc2_bias[None],
            fc1_bias.reshape(4, D // nf),
        ],
        axis=0,
    )
    small = gather(small, axis=1).astype(F32)
    gain1, gain2, shift1, shift2 = small[0:1], small[1:2], small[2:3], small[3:4]
    out_shift, fc2_shift = small[6:7], small[7:8]
    fc1_shift = lax.dynamic_slice_in_dim(small, 8 + c, 1, 0)
    q_shift = lax.dynamic_slice(small, (4, c * quarter), (1, quarter))
    v_shift = lax.dynamic_slice(small, (5, c * quarter), (1, quarter))
    qkv_shift = jnp.concatenate([q_shift, jnp.zeros_like(q_shift), v_shift], axis=1)

    rows_w = D // nf
    part_qkv = lax.dynamic_index_in_dim(
        qkv_weight.reshape(rows_w, 3, nc, quarter), c, 2, keepdims=False
    ).reshape(rows_w, 3 * quarter)
    w_qkv = gather(part_qkv)
    piece = rows_w // 4
    out_pairs = []
    for fs in range(nf):
        for j in range(nc):
            dst_c = fs // (nf // 4)
            dst_f = (fs % (nf // 4)) * 4 + j
            out_pairs.append((fs * nc + j, dst_f * nc + dst_c))
    out_back = [(b, a) for a, b in out_pairs]
    part_out = lax.ppermute(
        lax.dynamic_slice_in_dim(out_weight, c * piece, piece, 0), axes, out_pairs
    )
    w_out = gather(part_out)
    part_fc1 = lax.dynamic_index_in_dim(
        fc1_weight.reshape(rows_w, nf, 4, wide), c, 2, keepdims=False
    ).reshape(rows_w, D)
    w_fc1 = gather(part_fc1)
    part_fc2 = lax.dynamic_slice_in_dim(fc2_weight, c * wide, wide, 0)
    w_fc2 = gather(part_fc2)

    position = c * length + jnp.arange(length)
    g_all = []
    for i in range(n_img):
        keep = ((position < LIVE) & (slot_valid[i] > 0))[:, None]
        g = jnp.where(keep, out_grad[i], jnp.zeros((), BF16))
        g_all.append(spread(jnp.pad(g, ((0, PAD - length), (0, 0)))))

    saved = []
    for i in range(n_img):
        x = x_all[i].astype(F32)
        xhat1, inv1 = layer_norm(x)
        normed = (xhat1 * gain1 + shift1).astype(BF16)
        qkv = (dot(normed, w_qkv) + qkv_shift).astype(BF16)
        mask = x_all[i].reshape(4, PAD, D)[:, MASK_ROW, :PAD].reshape(1, 4 * PAD)
        bias = (1.0 - mask.astype(F32)) * NEG
        context = attention(qkv, bias)
        middle = x + all_rows(dot(context, w_out)) + out_shift
        xhat2, inv2 = layer_norm(middle)
        normed_mid = (xhat2 * gain2 + shift2).astype(BF16)
        pre = dot(normed_mid, w_fc1) + fc1_shift
        sig = jax.nn.sigmoid(1.702 * pre)
        hidden = (pre * sig).astype(BF16)
        res = own_rows(dot(hidden, w_fc2))
        result = (middle[:PAD] + res + fc2_shift).astype(BF16)[:length]
        saved.append((xhat1, inv1, normed, qkv, bias, context, middle, xhat2, inv2, normed_mid, pre, sig, hidden, result))

    grads = []
    for i in range(n_img):
        (xhat1, inv1, normed, qkv, bias, context, middle, xhat2, inv2, normed_mid, pre, sig, hidden, result) = saved[i]
        g = g_all[i]
        d_hidden = dot_nt(g, w_fc2)
        d_pre = d_hidden * (sig + 1.702 * pre * sig * (1.0 - sig))
        fc1_sum = jnp.sum(d_pre, axis=0, keepdims=True)
        d_pre_low = d_pre.astype(BF16)
        d_norm = all_rows(dot_nt(d_pre_low, w_fc1))
        d_mid = g.astype(F32) + norm_reverse(d_norm * gain2, xhat2, inv2)
        d_mid_low = d_mid.astype(BF16)
        d_context = dot_nt(d_mid_low, w_out).astype(BF16)
        bias_col = jnp.broadcast_to(bias.reshape(-1, 1), (4 * PAD, 128))
        dq, dk, dv, qv_sum = attention_back(qkv, d_context, bias_col)
        d_raw = jnp.concatenate([dq, dk, dv], axis=1)
        d_normed = own_rows(dot_nt(d_raw, w_qkv))
        d_tok = d_mid[:PAD] + norm_reverse(d_normed * gain1, xhat1[:PAD], inv1[:PAD])
        d_tok = d_tok.astype(BF16)[:length]
        own_norm = d_norm[:PAD]
        vectors = [
            jnp.sum(d_normed * xhat1[:PAD], axis=0, keepdims=True),
            jnp.sum(own_norm * xhat2[:PAD], axis=0, keepdims=True),
            jnp.sum(d_normed, axis=0, keepdims=True),
            jnp.sum(own_norm, axis=0, keepdims=True),
            jnp.sum(d_mid[:PAD], axis=0, keepdims=True),
            jnp.sum(g[:PAD].astype(F32), axis=0, keepdims=True),
        ]
        grads.append((d_pre_low, d_mid_low, d_raw, d_tok, vectors, fc1_sum, qv_sum))

    def over_images(lefts, rights):
        total = dot_tn(lefts[0], rights[0])
        for a, b in zip(lefts[1:], rights[1:]):
            total = total + dot_tn(a, b)
        return total

    p_fc2 = over_images([s[12] for s in saved], g_all)
    p_fc1 = over_images([s[9] for s in saved], [r[0] for r in grads])
    p_out = over_images([s[5] for s in saved], [r[1] for r in grads])
    p_qkv = over_images([s[2] for s in saved], [r[2] for r in grads])

    fc2_g = scatter(p_fc2.reshape(nf, -1, D), BF16)
    fc1_g = scatter(p_fc1.reshape(nf, -1, D), BF16)
    out_g = scatter(p_out.reshape(nf, -1, D), BF16)
    qkv_g = scatter(p_qkv.reshape(nf, -1, 3 * quarter), BF16)
    out_g = lax.ppermute(out_g.astype(BF16), axes, out_back)
    fc2_full = ctx_all(fc2_g.astype(BF16)).reshape(-1, D).astype(F32)
    fc1_full = (
        ctx_all(fc1_g.astype(BF16))
        .reshape(nc, rows_w, nf, wide)
        .transpose(1, 2, 0, 3)
        .reshape(rows_w, 4 * D)
        .astype(F32)
    )
    out_full = ctx_all(out_g).reshape(rows_w, D).astype(F32)
    qkv_full = (
        ctx_all(qkv_g.astype(BF16))
        .reshape(nc, rows_w, 3, quarter)
        .transpose(1, 2, 0, 3)
        .reshape(rows_w, 3 * D)
        .astype(F32)
    )

    vec = [sum(r[4][k] for r in grads) for k in range(6)]
    fc1_sum = sum(r[5] for r in grads)
    qv_sum = sum(r[6] for r in grads)
    here = (jnp.arange(D) // quarter == c)[None]
    qv_rows = jnp.where(here, jnp.tile(qv_sum[0:2], (1, nc)), 0.0)
    fc1_rows = jnp.where((jnp.arange(4) == c)[:, None], fc1_sum, 0.0)
    packed = jnp.concatenate(vec[0:4] + [qv_rows] + vec[4:6] + [fc1_rows], axis=0)
    packed = packed.reshape(12, nf, D // nf).transpose(1, 0, 2)
    packed = scatter(packed, F32)
    packed = packed + across(packed)
    packed = packed + core(packed)

    return (
        jnp.stack([s[13] for s in saved]),
        jnp.stack([r[3] for r in grads]),
        packed[0:2],
        packed[2:4],
        qkv_full,
        packed[4:6],
        out_full,
        packed[6],
        fc1_full,
        packed[8:12].reshape(-1),
        fc2_full,
        packed[7],
    )


def solution(mesh):
    in_specs = (
        P("fsdp", "ctx", None),
        P("fsdp", "ctx", None),
        P("fsdp", "ctx"),
        P("fsdp"),
        P(None, "fsdp"),
        P(None, "fsdp"),
        P("fsdp", None),
        P(None, "fsdp"),
        P("fsdp", None),
        P("fsdp"),
        P("fsdp", None),
        P("fsdp"),
        P("fsdp", None),
        P("fsdp"),
    )
    out_specs = (
        P("fsdp", "ctx", None),
        P("fsdp", "ctx", None),
        P(None, "fsdp"),
        P(None, "fsdp"),
        P("fsdp", None),
        P(None, "fsdp"),
        P("fsdp", None),
        P("fsdp"),
        P("fsdp", None),
        P("fsdp"),
        P("fsdp", None),
        P("fsdp"),
    )
    step = functools.partial(body, mesh.shape["fsdp"], mesh.shape["ctx"])
    return jax.shard_map(step, mesh=mesh, in_specs=in_specs, out_specs=out_specs, check_vma=False)
```

```python
import functools

import jax
import jax.numpy as jnp
from jax import lax
from jax.experimental import pallas as pl
from jax.experimental.pallas import tpu as pltpu
from jax.sharding import PartitionSpec as P

D = 1024
HEADS = 16
HEAD_DIM = 64
LIVE = 577
PAD = 160
MASK_ROW = 148
NEG = -1e30
F32 = jnp.float32
BF16 = jnp.bfloat16


def dot(a, b):
    return lax.dot_general(a, b, (((1,), (0,)), ((), ())), preferred_element_type=F32)


def dot_nt(a, b):
    return lax.dot_general(a, b, (((1,), (1,)), ((), ())), preferred_element_type=F32)


def dot_tn(a, b):
    return lax.dot_general(a, b, (((0,), (0,)), ((), ())), preferred_element_type=F32)


def layer_norm(values):
    centred = values - jnp.mean(values, axis=-1, keepdims=True)
    inverse = lax.rsqrt(jnp.mean(centred * centred, axis=-1, keepdims=True) + 1e-05)
    return centred * inverse, inverse


def norm_reverse(grad, normed, inverse):
    first = jnp.mean(grad, axis=-1, keepdims=True)
    second = jnp.mean(grad * normed, axis=-1, keepdims=True)
    return inverse * (grad - first - normed * second)


def attn_fwd_kernel(qkv_ref, bias_ref, o_ref):
    rows = qkv_ref.shape[0]
    lane = lax.broadcasted_iota(jnp.int32, (1, 128), 1)
    k = qkv_ref[:, 128:256]
    v = qkv_ref[:, 256:384]
    bias = bias_ref[...]
    for start in range(0, rows, 128):
        q = qkv_ref[start : start + 128, 0:128] * 0.125
        outs = []
        for h in range(2):
            qh = jnp.where((lane // 64) == h, q, jnp.zeros_like(q))
            s = dot_nt(qh, k) + bias
            top = jnp.max(s, axis=-1, keepdims=True)
            e = jnp.exp(s - top)
            total = jnp.sum(e, axis=-1, keepdims=True)
            p = (e * (1.0 / total)).astype(BF16)
            outs.append(dot(p, v))
        o_ref[start : start + 128, :] = jnp.where(lane < 64, outs[0], outs[1]).astype(BF16)


def attn_bwd_kernel(qkv_ref, g_ref, bias_ref, d_ref, sum_ref, dk_acc, dv_acc):
    rows = qkv_ref.shape[0]
    lane = lax.broadcasted_iota(jnp.int32, (1, 128), 1)
    k = qkv_ref[:, 128:256]
    v = qkv_ref[:, 256:384]
    bias = bias_ref[:, 0:1]
    qsum = jnp.zeros((1, 128), F32)
    for start in range(0, rows, 128):
        q = qkv_ref[start : start + 128, 0:128] * 0.125
        g = g_ref[start : start + 128, :]
        dqs, dks, dvs = [], [], []
        for h in range(2):
            mine = (lane // 64) == h
            qh = jnp.where(mine, q, jnp.zeros_like(q))
            gh = jnp.where(mine, g, jnp.zeros_like(g))
            s = dot_nt(k, qh) + bias
            top = jnp.max(s, axis=0, keepdims=True)
            e = jnp.exp(s - top)
            total = jnp.sum(e, axis=0, keepdims=True)
            p = e * (1.0 / total)
            dp = dot_nt(v, gh)
            delta = jnp.sum(p * dp, axis=0, keepdims=True)
            ds = (p * (dp - delta)).astype(BF16)
            dvs.append(dot(p.astype(BF16), gh))
            dks.append(dot(ds, qh))
            dqs.append(dot_tn(ds, k))
        dq = jnp.where(lane < 64, dqs[0], dqs[1]) * 0.125
        qsum = qsum + jnp.sum(dq, axis=0, keepdims=True)
        d_ref[start : start + 128, 0:128] = dq.astype(BF16)
        dk = dks[0] + dks[1]
        dv = dvs[0] + dvs[1]
        if start == 0:
            dk_acc[...] = dk
            dv_acc[...] = dv
        else:
            dk_acc[...] += dk
            dv_acc[...] += dv
    d_ref[:, 128:256] = dk_acc[...].astype(BF16)
    dv = dv_acc[...]
    d_ref[:, 256:384] = dv.astype(BF16)
    vsum = jnp.sum(dv, axis=0, keepdims=True)
    sum_ref[...] = jnp.concatenate([qsum, vsum, jnp.zeros((6, 128), F32)], axis=0)


def params(mib):
    return pltpu.CompilerParams(vmem_limit_bytes=mib << 20)


def cost(us):
    return pl.CostEstimate(flops=int(us * 1.1535e9), bytes_accessed=1024, transcendentals=0)


def attention(qkv, bias_row):
    rows = qkv.shape[0]
    return pl.pallas_call(
        attn_fwd_kernel,
        out_shape=jax.ShapeDtypeStruct((rows, 128), BF16),
        compiler_params=params(40),
        cost_estimate=cost(4.2),
        name="attn_fwd",
    )(qkv, bias_row)


def attention_back(pair, qkv, grad, bias_col):
    rows = grad.shape[0]
    full = lambda shape: pl.BlockSpec(shape, lambda i: (0, 0))
    return pl.pallas_call(
        attn_bwd_kernel,
        grid=(1,),
        in_specs=[
            full((rows, 384)),
            pl.BlockSpec((rows, 128), lambda i: (0, pair)),
            full((rows, 128)),
        ],
        out_specs=[full((rows, 384)), full((8, 128))],
        out_shape=[
            jax.ShapeDtypeStruct((rows, 384), BF16),
            jax.ShapeDtypeStruct((8, 128), F32),
        ],
        scratch_shapes=[pltpu.VMEM((rows, 128), F32)] * 2,
        compiler_params=params(48),
        cost_estimate=cost(6.0),
        name="attn_bwd",
    )(qkv, grad, bias_col)


CHUNK = 32
SC_SCATTER = True
SLOTS = (0, 2, 1, 3)


def prepare_kernel(n_img, *refs):
    slots, vec_ref, outs = refs[:4], refs[4], refs[5:]
    gain, add = vec_ref[0:1, :], vec_ref[2:3, :]
    for i in range(n_img):
        out_ref, bias_ref = outs[i], outs[n_img + i]
        for j, src in enumerate(slots):

            def step(k, carry):
                lo = pl.multiple_of(k * CHUNK, CHUNK)
                normed, _ = layer_norm(src[i, pl.ds(lo, CHUNK), :].astype(F32))
                out_ref[pl.ds(j * PAD + lo, CHUNK), :] = (normed * gain + add).astype(BF16)
                return carry

            lax.fori_loop(0, PAD // CHUNK, step, 0)
        masks = [src[i, MASK_ROW : MASK_ROW + 1, 0:PAD].astype(F32) for src in slots]
        bias_ref[...] = (1.0 - jnp.concatenate(masks, axis=1)) * NEG


def prepare(slots, small):
    n_img = slots[0].shape[0]
    out = pl.pallas_call(
        functools.partial(prepare_kernel, n_img),
        out_shape=[jax.ShapeDtypeStruct((4 * PAD, D), BF16)] * n_img
        + [jax.ShapeDtypeStruct((1, 4 * PAD), F32)] * n_img,
        compiler_params=params(40),
        cost_estimate=cost(6.0),
        name="prepare",
    )(*slots, small)
    return out[:n_img], out[n_img:]


def stack_kernel(n_img, *refs):
    slots, outs = refs[:4], refs[4:]
    for i in range(n_img):
        for j, src in enumerate(slots):
            outs[i][j * PAD : j * PAD + PAD, :] = src[i]


def stack_rows(slots):
    n_img = slots[0].shape[0]
    return pl.pallas_call(
        functools.partial(stack_kernel, n_img),
        out_shape=[jax.ShapeDtypeStruct((4 * PAD, D), BF16)] * n_img,
        compiler_params=params(32),
        cost_estimate=cost(2.0),
        name="stack_rows",
    )(*slots)


def middle_kernel(*refs):
    slots, (a_ref, b_ref, vec_ref, mid_ref, out_ref) = refs[:4], refs[4:]
    shift, gain, add = vec_ref[6:7, :], vec_ref[1:2, :], vec_ref[3:4, :]

    for j, src in enumerate(slots):
        part_ref = a_ref if j < 2 else b_ref

        def step(i, carry):
            lo = pl.multiple_of(i * CHUNK, CHUNK)
            at = pl.ds(j * PAD + lo, CHUNK)
            m = src[0, pl.ds(lo, CHUNK), :].astype(F32) + shift
            m = m + part_ref[pl.ds((j % 2) * PAD + lo, CHUNK), :].astype(F32)
            mid_ref[at, :] = m
            normed, _ = layer_norm(m)
            out_ref[at, :] = (normed * gain + add).astype(BF16)
            return carry

        lax.fori_loop(0, PAD // CHUNK, step, 0)


def middle_rows(image, slots, a, b, small):
    rows = 4 * PAD
    piece = pl.BlockSpec((1, PAD, D), lambda i: (image, 0, 0))
    full = lambda shape: pl.BlockSpec(shape, lambda i: (0, 0))
    return pl.pallas_call(
        middle_kernel,
        grid=(1,),
        in_specs=[piece] * 4 + [full(a.shape), full(b.shape), full(small.shape)],
        out_specs=[full((rows, D)), full((rows, D))],
        out_shape=[
            jax.ShapeDtypeStruct((rows, D), F32),
            jax.ShapeDtypeStruct((rows, D), BF16),
        ],
        compiler_params=params(32),
        cost_estimate=cost(2.4),
        name="middle",
    )(*slots, a, b, small)


def middle_back_kernel(mid_ref, a_ref, b_ref, g_ref, vec_ref, low_ref, own_ref, sum_ref):
    gain = vec_ref[1:2, :]
    half = a_ref.shape[0]

    def rows(src, base, lo):
        at = pl.ds(base + lo, CHUNK)
        normed, inverse = layer_norm(mid_ref[at, :])
        t = src[pl.ds(lo, CHUNK), :].astype(F32)
        g = g_ref[at, :].astype(F32)
        d = g + norm_reverse(t * gain, normed, inverse)
        low_ref[at, :] = d.astype(BF16)
        return normed, t, g, d

    def own(i, carry):
        lo = pl.multiple_of(i * CHUNK, CHUNK)
        normed, t, g, d = rows(a_ref, 0, lo)
        own_ref[pl.ds(lo, CHUNK), :] = d
        new = [jnp.sum(v, axis=0, keepdims=True) for v in (t * normed, t, d, g)]
        return tuple(c + n for c, n in zip(carry, new))

    zero = jnp.zeros((1, D), F32)
    sums = lax.fori_loop(0, PAD // CHUNK, own, (zero,) * 4)

    def other(src, base, first):
        def step(i, carry):
            rows(src, base, pl.multiple_of(i * CHUNK, CHUNK))
            return carry

        lax.fori_loop(first, half // CHUNK, step, 0, unroll=2 if first == 0 else 1)

    other(a_ref, 0, PAD // CHUNK)
    other(b_ref, half, 0)
    sum_ref[...] = jnp.concatenate(list(sums) + [jnp.zeros((4, D), F32)], axis=0)


def middle_back(mid, a, b, g, small):
    rows = mid.shape[0]
    return pl.pallas_call(
        middle_back_kernel,
        out_shape=[
            jax.ShapeDtypeStruct((rows, D), BF16),
            jax.ShapeDtypeStruct((PAD, D), F32),
            jax.ShapeDtypeStruct((8, D), F32),
        ],
        compiler_params=params(32),
        cost_estimate=cost(4.0),
        name="middle_back",
    )(mid, a, b, g, small)


def pieces_of(length):
    return [(lo, min(CHUNK, length - lo)) for lo in range(0, length, CHUNK)]


def result_kernel(n_img, *refs):
    mids, mine, got = refs[:n_img], refs[n_img : 2 * n_img], refs[2 * n_img : 3 * n_img]
    vec_ref, out_ref = refs[3 * n_img :]
    shift = vec_ref[7:8, :]
    for i in range(n_img):
        for lo, n in pieces_of(out_ref.shape[1]):
            at = slice(lo, lo + n)
            total = mids[i][at, :] + mine[i][at, :].astype(F32) + got[i][at, :].astype(F32)
            out_ref[i, at, :] = (total + shift).astype(BF16)


def result_rows(length, mids, mine, got, small):
    n_img = len(mids)
    spec = pl.BlockSpec((PAD, D), lambda i: (0, 0))
    return pl.pallas_call(
        functools.partial(result_kernel, n_img),
        grid=(1,),
        in_specs=[spec] * (3 * n_img) + [pl.BlockSpec(small.shape, lambda i: (0, 0))],
        out_specs=pl.BlockSpec((n_img, length, D), lambda i: (0, 0, 0)),
        out_shape=jax.ShapeDtypeStruct((n_img, length, D), BF16),
        compiler_params=params(32),
        cost_estimate=cost(1.5),
        name="result",
    )(*mids, *mine, *got, small)


def tokens_back_kernel(n_img, x_ref, *refs):
    dmid, mine, got = refs[:n_img], refs[n_img : 2 * n_img], refs[2 * n_img : 3 * n_img]
    vec_ref, out_ref, sum_ref = refs[3 * n_img :]
    gain = vec_ref[0:1, :]
    first = jnp.zeros((1, D), F32)
    second = jnp.zeros((1, D), F32)
    for i in range(n_img):
        for lo, n in pieces_of(out_ref.shape[1]):
            at = slice(lo, lo + n)
            normed, inverse = layer_norm(x_ref[i, at, :].astype(F32))
            u = mine[i][at, :].astype(F32) + got[i][at, :].astype(F32)
            first = first + jnp.sum(u * normed, axis=0, keepdims=True)
            second = second + jnp.sum(u, axis=0, keepdims=True)
            d = dmid[i][at, :] + norm_reverse(u * gain, normed, inverse)
            out_ref[i, at, :] = d.astype(BF16)
    sum_ref[...] = jnp.concatenate([first, second, jnp.zeros((6, D), F32)], axis=0)


def tokens_back(length, x, dmid, mine, got, small):
    n_img = len(dmid)
    spec = pl.BlockSpec((PAD, D), lambda i: (0, 0))
    return pl.pallas_call(
        functools.partial(tokens_back_kernel, n_img),
        grid=(1,),
        in_specs=[pl.BlockSpec(x.shape, lambda i: (0, 0, 0))]
        + [spec] * (3 * n_img)
        + [pl.BlockSpec(small.shape, lambda i: (0, 0))],
        out_specs=[
            pl.BlockSpec((n_img, length, D), lambda i: (0, 0, 0)),
            pl.BlockSpec((8, D), lambda i: (0, 0)),
        ],
        out_shape=[
            jax.ShapeDtypeStruct((n_img, length, D), BF16),
            jax.ShapeDtypeStruct((8, D), F32),
        ],
        compiler_params=params(32),
        cost_estimate=cost(2.0),
        name="tokens_back",
    )(x, *dmid, *mine, *got, small)


def weave_kernel(bit_ref, a_ref, b_ref, o_ref):
    up = bit_ref[0]
    for i in range(a_ref.shape[0]):
        o_ref[i, up] = a_ref[i]
        o_ref[i, 1 - up] = b_ref[i]


def weave(bit, a, b):
    m, r, w = a.shape
    if r % 8 or w % 128:
        up = bit == 1
        low, high = jnp.where(up, b, a), jnp.where(up, a, b)
        return jnp.stack([low, high], axis=1).reshape(2 * m, r, w)
    vmem = pl.BlockSpec(memory_space=pltpu.VMEM)
    out = pl.pallas_call(
        weave_kernel,
        in_specs=[pl.BlockSpec(memory_space=pltpu.SMEM), vmem, vmem],
        out_specs=vmem,
        out_shape=jax.ShapeDtypeStruct((m, 2, r, w), a.dtype),
        compiler_params=params(24),
        cost_estimate=cost(0.5 + m * r * w * 2e-6),
        name="weave",
    )(bit.astype(jnp.int32).reshape(1), a, b)
    return out.reshape(2 * m, r, w)


def place_qkv_kernel(c_ref, *refs):
    out_ref = refs[-1]
    c = c_ref[0]
    for j, ref in enumerate(refs[:-1]):
        pair, slot = j // 4, j % 4
        for k in range(3):
            at = pl.multiple_of(k * D + (c ^ SLOTS[slot]) * 256 + pair * 128, 128)
            out_ref[:, pl.ds(at, 128)] = ref[:, k * 128 : k * 128 + 128].astype(F32)


def place_rest_kernel(r, wide, piece, c_ref, *refs):
    slots, (fc2_ref, fc1_ref, out_ref) = refs[:4], refs[4:]
    c = c_ref[0]
    for slot, ref in enumerate(slots):
        q = c ^ SLOTS[slot]
        fc2_ref[pl.ds(pl.multiple_of(q * wide, 8), wide), :] = ref[0:wide, :].astype(F32)
        for f in range(D // wide):
            at = pl.multiple_of(f * 4 * wide + q * wide, 128)
            fc1_ref[:, pl.ds(at, wide)] = ref[wide : wide + r, f * wide : (f + 1) * wide].astype(F32)
        out_ref[pl.ds(pl.multiple_of(q * piece, 8), piece), :] = ref[wide + r :, :].astype(F32)


def in_order(c, slots):
    own, y, core, both = slots
    odd = c % 2 == 1
    low = [jnp.where(odd, core, own), jnp.where(odd, own, core)]
    high = [jnp.where(odd, both, y), jnp.where(odd, y, both)]
    up = c // 2 == 1
    return jnp.stack(
        [jnp.where(up, b, a) for a, b in zip(low, high)]
        + [jnp.where(up, a, b) for a, b in zip(low, high)]
    )


def place_qkv(c, pairs):
    r = pairs[0][0].shape[0]
    smem = pl.BlockSpec(memory_space=pltpu.SMEM)
    vmem = pl.BlockSpec(memory_space=pltpu.VMEM)
    flat = [v for slots in pairs for v in slots]
    return pl.pallas_call(
        place_qkv_kernel,
        in_specs=[smem] + [vmem] * len(flat),
        out_specs=vmem,
        out_shape=jax.ShapeDtypeStruct((r, 3 * D), F32),
        compiler_params=params(24),
        cost_estimate=cost(1.5),
        name="place_qkv",
    )(c.astype(jnp.int32).reshape(1), *flat)


def place_rest(c, r, wide, piece, slots):
    if wide % 128 or piece % 8:
        full = in_order(c, slots).astype(F32)
        fc2 = full[:, :wide].reshape(-1, D)
        fc1 = full[:, wide : wide + r].reshape(4, r, D // wide, wide)
        fc1 = fc1.transpose(1, 2, 0, 3).reshape(r, 4 * D)
        return fc2, fc1, full[:, wide + r :].reshape(-1, D)
    smem = pl.BlockSpec(memory_space=pltpu.SMEM)
    vmem = pl.BlockSpec(memory_space=pltpu.VMEM)
    return pl.pallas_call(
        functools.partial(place_rest_kernel, r, wide, piece),
        in_specs=[smem] + [vmem] * 4,
        out_specs=[vmem] * 3,
        out_shape=[
            jax.ShapeDtypeStruct((4 * wide, D), F32),
            jax.ShapeDtypeStruct((r, 4 * D), F32),
            jax.ShapeDtypeStruct((4 * piece, D), F32),
        ],
        compiler_params=params(32),
        cost_estimate=cost(4.0),
        name="place_rest",
    )(c.astype(jnp.int32).reshape(1), *slots)


def gate(value, *after):
    return lax.optimization_barrier((value,) + after)[0]


def body(
    nf,
    nc,
    tokens,
    out_grad,
    key_mask,
    slot_valid,
    norm_gains,
    norm_shifts,
    qkv_weight,
    qv_bias,
    out_weight,
    out_bias,
    fc1_weight,
    fc1_bias,
    fc2_weight,
    fc2_bias,
):
    f = lax.axis_index("fsdp")
    c = lax.axis_index("ctx")
    axes = ("fsdp", "ctx")
    bits = []
    while (1 << len(bits)) < nf:
        bits.append(1 << len(bits))

    def swap(v, df, dc):
        pairs = [(i * nc + j, (i ^ df) * nc + (j ^ dc)) for i in range(nf) for j in range(nc)]
        return lax.ppermute(v, axes, pairs)

    def core(v):
        return swap(v, 0, 1)

    def across(v):
        return swap(v, 0, 2)

    def gather_steps(shard):
        held = [shard[None]]
        for b in reversed(bits):
            buf = held[-1]
            held.append(weave((f // b) % 2, buf, swap(buf, b, 0)))
        return held

    def flat(buf):
        return buf.reshape((-1,) + buf.shape[2:])

    def scatter(full, low):
        for b in bits:
            v = full.reshape((full.shape[0] // 2, 2) + full.shape[1:])
            up = (f // b) % 2
            send = lax.dynamic_index_in_dim(v, 1 - up, 1, keepdims=False).astype(low)
            keep = lax.dynamic_index_in_dim(v, up, 1, keepdims=False)
            full = keep + swap(send, b, 0).astype(F32)
        return full[0]

    def slots_of(v):
        y = across(v)
        return [v, y, core(v), core(y)]

    n_img, length = tokens.shape[0], tokens.shape[1]
    quarter = D // nc
    rows_w = D // nf
    wide = 4 * D // nf // nc
    piece = rows_w // nc
    half = 2 * PAD

    by_pair = lax.dynamic_index_in_dim(
        qkv_weight.reshape(rows_w, 3, nc, 2, 128), c, 2, keepdims=False
    )
    qkv_held = [gather_steps(by_pair[:, :, p, :].reshape(rows_w, 384)) for p in range(2)]
    w_qkv = [flat(held[-1]) for held in qkv_held]

    small = jnp.concatenate(
        [
            norm_gains,
            norm_shifts,
            qv_bias,
            out_bias[None],
            fc2_bias[None],
            fc1_bias.reshape(4, D // nf),
        ],
        axis=0,
    )
    buf = small[None]
    for b in reversed(bits):
        other = swap(buf, b, 0)
        up = (f // b) % 2 == 1
        low, high = jnp.where(up, other, buf), jnp.where(up, buf, other)
        buf = jnp.stack([low, high], axis=1).reshape((2 * buf.shape[0],) + small.shape)
    small = buf.transpose(1, 0, 2).reshape(12, D).astype(F32)
    fc1_shift = lax.dynamic_slice_in_dim(small, 8 + c, 1, 0)
    qkv_shift = []
    for p in range(2):
        q_shift = lax.dynamic_slice(small, (4, c * quarter + p * 128), (1, 128))
        v_shift = lax.dynamic_slice(small, (5, c * quarter + p * 128), (1, 128))
        qkv_shift.append(jnp.concatenate([q_shift, jnp.zeros_like(q_shift), v_shift], axis=1))

    mask_rows = jnp.pad(key_mask.astype(BF16), ((0, 0), (0, D - length)))[:, None, :]
    x_own = jnp.concatenate(
        [tokens, mask_rows, jnp.zeros((n_img, PAD - length - 1, D), BF16)], axis=1
    )
    x_slots = slots_of(x_own)
    position = c * length + jnp.arange(length)
    keep = (position < LIVE)[None, :] & (slot_valid[:, None] > 0)
    g_own = jnp.where(keep[:, :, None], out_grad, jnp.zeros((), BF16))
    g_own = jnp.pad(g_own, ((0, 0), (0, PAD - length), (0, 0)))
    g_slots = slots_of(gate(g_own, x_slots[1]))
    g_all = stack_rows(g_slots)

    out_pairs = []
    for fs in range(nf):
        for j in range(nc):
            dst_f = (fs % (nf // 4)) * 4 + j
            out_pairs.append((fs * nc + j, dst_f * nc + fs // (nf // 4)))
    out_back = [(b, a) for a, b in out_pairs]
    out_part = lax.dynamic_slice_in_dim(out_weight, c * piece, piece, 0)
    out_part = lax.ppermute(gate(out_part, qkv_held[0][1]), axes, out_pairs)
    out_held = gather_steps(gate(out_part, qkv_held[1][1]))
    fc1_part = lax.dynamic_index_in_dim(
        fc1_weight.reshape(rows_w, nf, 4, wide), c, 2, keepdims=False
    ).reshape(rows_w, D)
    fc1_held = gather_steps(gate(fc1_part, out_held[1], qkv_held[1][2]))
    fc2_part = lax.dynamic_slice_in_dim(fc2_weight, c * wide, wide, 0)
    fc2_held = gather_steps(gate(fc2_part, fc1_held[1]))
    w_out, w_fc1, w_fc2 = flat(out_held[-1]), flat(fc1_held[-1]), flat(fc2_held[-1])

    images = range(n_img)
    normed, bias = prepare(x_slots, small)
    qkv = [[None] * n_img for _ in range(2)]
    contexts = [[None] * n_img for _ in range(2)]

    def reduce_send(left, weight, back=False):
        product = dot_nt if back else dot
        return product(left[half:], weight).astype(BF16)

    def reduce_mine(left, weight, got, back=False):
        product = dot_nt if back else dot
        return (product(left[:half], weight) + got.astype(F32)).astype(BF16)

    def finish(mine):
        got = across(mine)
        got = jnp.concatenate([got[PAD:], got[:PAD]], axis=0)
        mine = (mine.astype(F32) + got.astype(F32)).astype(BF16)
        return mine, core(mine)

    context, sums1 = [None] * n_img, [None] * n_img
    last = None
    for p in range(2):
        for i in images:
            qkv[p][i] = (dot(normed[i], w_qkv[p]) + qkv_shift[p]).astype(BF16)
            ready = qkv[p][i] if last is None else gate(qkv[p][i], last)
            contexts[p][i] = attention(ready, bias[i])
            last = None
            if p == 1:
                context[i] = jnp.concatenate([contexts[0][i], contexts[1][i]], axis=1)
                send = reduce_send(context[i], w_out)
                mine = reduce_mine(context[i], w_out, core(send))
                sums1[i] = finish(mine)
                last = mine

    middle, normed_mid, hidden, d_pre_low, fc1_sum, sums2 = [], [], [], [], [], []
    for i in images:
        mid, low = middle_rows(i, x_slots, sums1[i][0], sums1[i][1], small)
        middle.append(mid)
        normed_mid.append(low)
        pre = dot(low, w_fc1) + fc1_shift
        sig = jax.nn.sigmoid(1.702 * pre)
        hidden.append((pre * sig).astype(BF16))
        d_hidden = dot_nt(g_all[i], w_fc2)
        d_pre = d_hidden * (sig + 1.702 * pre * sig * (1.0 - sig))
        fc1_sum.append(jnp.sum(d_pre, axis=0, keepdims=True))
        d_pre_low.append(d_pre.astype(BF16))
        send = reduce_send(d_pre_low[i], w_fc1, True)
        mine = reduce_mine(d_pre_low[i], w_fc1, core(send), True)
        sums2.append(finish(mine))
        last = mine

    def over_images(lefts, rights):
        total = dot_tn(lefts[0], rights[0])
        for a, b in zip(lefts[1:], rights[1:]):
            total = total + dot_tn(a, b)
        return total

    p_fc2 = over_images([gate(h, last) for h in hidden], g_all)
    p_fc1 = over_images(normed_mid, d_pre_low)
    if SC_SCATTER:
        both = jnp.concatenate([p_fc2.astype(BF16), p_fc1.astype(BF16)], axis=1)
        both = lax.psum_scatter(both, "fsdp", scatter_dimension=0, tiled=True)
        fc2_g, fc1_g = both[:, :D], both[:, D:]
    else:
        fc2_g = scatter(p_fc2.reshape(nf, -1, D), BF16).astype(BF16)
        fc1_g = scatter(p_fc1.reshape(nf, -1, D), BF16).astype(BF16)

    mines, gots = [], []
    for i in images:
        send = reduce_send(gate(hidden[i], sums2[-1][0]), w_fc2)
        mine = reduce_mine(hidden[i], w_fc2, core(send))
        mines.append(mine)
        gots.append(across(mine[PAD:]))
    result = result_rows(length, middle, mines, gots, small)

    d_mid_low, d_mid_own, mid_sums, d_context = [], [], [], []
    for i in images:
        low, own, sums = middle_back(middle[i], sums2[i][0], sums2[i][1], g_all[i], small)
        d_mid_low.append(low)
        d_mid_own.append(own)
        mid_sums.append(sums)
        d_context.append(dot_nt(low, w_out).astype(BF16))
    p_out = over_images(context, d_mid_low)
    out_g = scatter(p_out.reshape(nf, -1, D), BF16).astype(BF16)
    out_g = lax.ppermute(out_g, axes, out_back)

    d_raw = [[None] * n_img for _ in range(2)]
    qv_sum = []
    qkv_slots = []
    for p in range(2):
        sums = []
        for i in images:
            bias_col = jnp.broadcast_to(bias[i].reshape(-1, 1), (4 * PAD, 128))
            d_raw[p][i], s = attention_back(p, qkv[p][i], d_context[i], bias_col)
            sums.append(s)
        qv_sum.append(sum(sums[1:], sums[0]))
        lefts = normed if p == 0 else [gate(normed[0], result)] + list(normed[1:])
        p_qkv = over_images(lefts, d_raw[p])
        qkv_g = scatter(p_qkv.reshape(nf, -1, 384), BF16).astype(BF16)
        qkv_slots.append(slots_of(qkv_g))

    mines, gots = [], []
    for i in images:
        parts = [d_raw[p][i] for p in range(2)]
        send = sum(dot_nt(parts[p][half:], w_qkv[p]) for p in range(2)).astype(BF16)
        mine = sum(dot_nt(parts[p][:half], w_qkv[p]) for p in range(2))
        mine = (mine + core(send).astype(F32)).astype(BF16)
        mines.append(mine)
        gots.append(across(mine[PAD:]))
    token_gradient, tok_sums = tokens_back(length, x_own, d_mid_own, mines, gots, small)

    rest = jnp.concatenate([fc2_g, fc1_g, out_g], axis=0)
    fc2_full, fc1_full, out_full = place_rest(c, rows_w, wide, piece, slots_of(rest))
    qkv_full = place_qkv(c, qkv_slots)

    mid_sum = sum(mid_sums[1:], mid_sums[0])
    fc1_rows = jnp.where((jnp.arange(4) == c)[:, None], sum(fc1_sum[1:], fc1_sum[0]), 0.0)
    here = (jnp.arange(D) // quarter == c)[None]
    qv_rows = jnp.concatenate([s[0:2] for s in qv_sum], axis=1)
    qv_rows = jnp.where(here, jnp.tile(qv_rows, (1, nc)), 0.0)
    packed = jnp.concatenate(
        [tok_sums[0:1], mid_sum[0:1], tok_sums[1:2], mid_sum[1:2], qv_rows, mid_sum[2:4], fc1_rows],
        axis=0,
    )
    packed = packed.reshape(12, nf, D // nf).transpose(1, 0, 2)
    packed = scatter(packed, F32)
    packed = packed + across(packed)
    packed = packed + core(packed)

    return (
        result,
        token_gradient,
        packed[0:2],
        packed[2:4],
        qkv_full,
        packed[4:6],
        out_full,
        packed[6],
        fc1_full,
        packed[8:12].reshape(-1),
        fc2_full,
        packed[7],
    )


def solution(mesh):
    in_specs = (
        P("fsdp", "ctx", None),
        P("fsdp", "ctx", None),
        P("fsdp", "ctx"),
        P("fsdp"),
        P(None, "fsdp"),
        P(None, "fsdp"),
        P("fsdp", None),
        P(None, "fsdp"),
        P("fsdp", None),
        P("fsdp"),
        P("fsdp", None),
        P("fsdp"),
        P("fsdp", None),
        P("fsdp"),
    )
    out_specs = (
        P("fsdp", "ctx", None),
        P("fsdp", "ctx", None),
        P(None, "fsdp"),
        P(None, "fsdp"),
        P("fsdp", None),
        P(None, "fsdp"),
        P("fsdp", None),
        P("fsdp"),
        P("fsdp", None),
        P("fsdp"),
        P("fsdp", None),
        P("fsdp"),
    )
    step = functools.partial(body, mesh.shape["fsdp"], mesh.shape["ctx"])
    return jax.shard_map(step, mesh=mesh, in_specs=in_specs, out_specs=out_specs, check_vma=False)
```

```python
import functools

import jax
import jax.numpy as jnp
from jax import lax
from jax.experimental import pallas as pl
from jax.experimental.pallas import tpu as pltpu
from jax.sharding import PartitionSpec as P

D = 1024
HEADS = 16
HEAD_DIM = 64
LIVE = 577
PAD = 160
MASK_ROW = 148
NEG = -1e30
F32 = jnp.float32
BF16 = jnp.bfloat16


def dot(a, b):
    return lax.dot_general(a, b, (((1,), (0,)), ((), ())), preferred_element_type=F32)


def dot_nt(a, b):
    return lax.dot_general(a, b, (((1,), (1,)), ((), ())), preferred_element_type=F32)


def dot_tn(a, b):
    return lax.dot_general(a, b, (((0,), (0,)), ((), ())), preferred_element_type=F32)


def layer_norm(values):
    centred = values - jnp.mean(values, axis=-1, keepdims=True)
    inverse = lax.rsqrt(jnp.mean(centred * centred, axis=-1, keepdims=True) + 1e-05)
    return centred * inverse, inverse


def norm_reverse(grad, normed, inverse):
    first = jnp.mean(grad, axis=-1, keepdims=True)
    second = jnp.mean(grad * normed, axis=-1, keepdims=True)
    return inverse * (grad - first - normed * second)


def attn_fwd_kernel(qkv_ref, bias_ref, o_ref, lse_ref):
    lane = lax.broadcasted_iota(jnp.int32, (1, 128), 1)
    q = qkv_ref[:, 0:128] * 0.125
    k = qkv_ref[:, 128:256]
    v = qkv_ref[:, 256:384]
    bias = bias_ref[:, 0:1]
    outs = []
    lse_ref[2:8, :] = jnp.zeros((6, lse_ref.shape[1]), F32)
    for h in range(2):
        qh = jnp.where((lane // 64) == h, q, jnp.zeros_like(q))
        s = dot_nt(k, qh) + bias
        top = jnp.max(s, axis=0, keepdims=True)
        e = jnp.exp(s - top)
        total = jnp.sum(e, axis=0, keepdims=True)
        p = (e * (1.0 / total)).astype(BF16)
        lse_ref[h : h + 1, :] = top + jnp.log(total)
        outs.append(dot_tn(p, v))
    o_ref[...] = jnp.where(lane < 64, outs[0], outs[1]).astype(BF16)


def attn_bwd_kernel(qkv_ref, g_ref, bias_ref, lse_ref, d_ref, sum_ref, dq_acc, dk_acc, dv_acc):
    lane = lax.broadcasted_iota(jnp.int32, (1, 128), 1)
    dk_acc[...] = jnp.zeros_like(dk_acc)
    dv_acc[...] = jnp.zeros_like(dv_acc)

    def head(h, carry):
        q = qkv_ref[:, 0:128] * 0.125
        k = qkv_ref[:, 128:256]
        v = qkv_ref[:, 256:384]
        g = g_ref[...]
        mine = (lane // 64) == h
        qh = jnp.where(mine, q, jnp.zeros_like(q))
        gh = jnp.where(mine, g, jnp.zeros_like(g))
        s = dot_nt(k, qh) + bias_ref[:, 0:1]
        p = jnp.exp(s - lse_ref[pl.ds(h, 1), :])
        dp = dot_nt(v, gh)
        delta = jnp.sum(p * dp, axis=0, keepdims=True)
        ds = (p * (dp - delta)).astype(BF16)
        dv_acc[...] += dot(p.astype(BF16), gh)
        dk_acc[...] += dot(ds, qh)
        dq_acc[...] = jnp.where(mine, dot_tn(ds, k) * 0.125, dq_acc[...])
        return carry

    lax.fori_loop(0, 2, head, 0)
    dq = dq_acc[...]
    dv = dv_acc[...]
    d_ref[:, 0:128] = dq.astype(BF16)
    d_ref[:, 128:256] = dk_acc[...].astype(BF16)
    d_ref[:, 256:384] = dv.astype(BF16)
    sums = [jnp.sum(x, axis=0, keepdims=True) for x in (dq, dv)]
    sum_ref[...] = jnp.concatenate(sums + [jnp.zeros((6, 128), F32)], axis=0)


def params(mib):
    return pltpu.CompilerParams(vmem_limit_bytes=mib << 20)


def cost(us):
    return pl.CostEstimate(flops=int(us * 1e7), bytes_accessed=1024, transcendentals=0)


def attention(n_img, qkv, bias_col):
    rows = qkv.shape[0] // n_img
    spec = lambda w: pl.BlockSpec((rows, w), lambda i: (i, 0))
    return pl.pallas_call(
        attn_fwd_kernel,
        grid=(n_img,),
        in_specs=[spec(384), spec(128)],
        out_specs=[spec(128), pl.BlockSpec((8, rows), lambda i: (i, 0))],
        out_shape=[
            jax.ShapeDtypeStruct((n_img * rows, 128), BF16),
            jax.ShapeDtypeStruct((n_img * 8, rows), F32),
        ],
        compiler_params=params(48),
        cost_estimate=cost(4.0),
        name="attn_fwd",
    )(qkv, bias_col)


def attention_back(pair, image, qkv, grad, bias_col, lse):
    rows = grad.shape[0]
    full = lambda shape: pl.BlockSpec(shape, lambda i: (0, 0))
    return pl.pallas_call(
        attn_bwd_kernel,
        grid=(1,),
        in_specs=[
            pl.BlockSpec((rows, 384), lambda i: (image, 0)),
            pl.BlockSpec((rows, 128), lambda i: (0, pair)),
            pl.BlockSpec((rows, 128), lambda i: (image, 0)),
            pl.BlockSpec((8, rows), lambda i: (image, 0)),
        ],
        out_specs=[full((rows, 384)), full((8, 128))],
        out_shape=[
            jax.ShapeDtypeStruct((rows, 384), BF16),
            jax.ShapeDtypeStruct((8, 128), F32),
        ],
        scratch_shapes=[pltpu.VMEM((rows, 128), F32)] * 3,
        compiler_params=params(48),
        cost_estimate=cost(3.7),
        name="attn_bwd",
    )(qkv, grad, bias_col, lse)


CHUNK = 32
SLOTS = (0, 2, 1, 3)


def prepare_kernel(n_img, *refs):
    slots, (vec_ref, out_ref, bias_ref) = refs[:4], refs[4:]
    gain, add = vec_ref[0:1, :], vec_ref[2:3, :]
    row = lax.broadcasted_iota(jnp.int32, (PAD, PAD), 0)
    lane = lax.broadcasted_iota(jnp.int32, (PAD, PAD), 1)

    def image(i, carry):
        for j, src in enumerate(slots):
            base = pl.multiple_of(i * 4 * PAD + j * PAD, PAD)
            for lo in range(0, PAD, CHUNK):
                normed, _ = layer_norm(src[i, lo : lo + CHUNK, :].astype(F32))
                out_ref[pl.ds(base + lo, CHUNK), :] = (normed * gain + add).astype(BF16)
            mask = src[i, MASK_ROW : MASK_ROW + 1, 0:PAD].astype(F32)
            hidden = jnp.where(row == lane, (1.0 - mask) * NEG, 0.0)
            hidden = jnp.sum(hidden, axis=1, keepdims=True)
            bias_ref[pl.ds(base, PAD), :] = jnp.broadcast_to(hidden, (PAD, 128))
        return carry

    lax.fori_loop(0, n_img, image, 0)


def prepare(slots, small):
    n_img = slots[0].shape[0]
    rows = n_img * 4 * PAD
    return pl.pallas_call(
        functools.partial(prepare_kernel, n_img),
        out_shape=[
            jax.ShapeDtypeStruct((rows, D), BF16),
            jax.ShapeDtypeStruct((rows, 128), F32),
        ],
        compiler_params=params(40),
        cost_estimate=cost(4.2),
        name="prepare",
    )(*slots, small)


def stack_kernel(n_img, *refs):
    slots, out_ref = refs[:4], refs[4]
    for i in range(n_img):
        for j, src in enumerate(slots):
            base = (4 * i + j) * PAD
            out_ref[base : base + PAD, :] = src[i]


def stack_rows(slots):
    n_img = slots[0].shape[0]
    return pl.pallas_call(
        functools.partial(stack_kernel, n_img),
        out_shape=jax.ShapeDtypeStruct((n_img * 4 * PAD, D), BF16),
        compiler_params=params(32),
        cost_estimate=cost(2.0),
        name="stack_rows",
    )(*slots)


def middle_kernel(n_img, *refs):
    slots, parts = refs[:4], refs[4 : 4 + 4 * n_img]
    vec_ref, mid_ref, out_ref = refs[4 + 4 * n_img :]
    shift, gain, add = vec_ref[6:7, :], vec_ref[1:2, :], vec_ref[3:4, :]
    for i in range(n_img):
        mine, got = parts[4 * i], parts[4 * i + 1]
        rest = parts[4 * i + 2 : 4 * i + 4]
        for j, src in enumerate(slots):
            for lo in range(0, PAD, CHUNK):
                near = slice(lo, lo + CHUNK)
                if j < 2:
                    far = slice((1 - j) * PAD + lo, (1 - j) * PAD + lo + CHUNK)
                    own = slice(j * PAD + lo, j * PAD + lo + CHUNK)
                    part = mine[own, :].astype(F32) + got[far, :].astype(F32)
                    part = part.astype(BF16).astype(F32)
                else:
                    part = rest[j - 2][near, :].astype(F32)
                at = slice((4 * i + j) * PAD + lo, (4 * i + j) * PAD + lo + CHUNK)
                m = src[i, near, :].astype(F32) + shift + part
                mid_ref[at, :] = m
                normed, _ = layer_norm(m)
                out_ref[at, :] = (normed * gain + add).astype(BF16)


def middle_rows(slots, parts, small):
    n_img = slots[0].shape[0]
    rows = n_img * 4 * PAD
    return pl.pallas_call(
        functools.partial(middle_kernel, n_img),
        out_shape=[
            jax.ShapeDtypeStruct((rows, D), F32),
            jax.ShapeDtypeStruct((rows, D), BF16),
        ],
        compiler_params=params(40),
        cost_estimate=cost(5.0),
        name="middle",
    )(*slots, *parts, small)


def middle_back_kernel(mid_ref, a_ref, b0_ref, b1_ref, g_ref, vec_ref, low_ref, own_ref, sum_ref):
    gain = vec_ref[1:2, :]
    sums = [jnp.zeros((1, D), F32)] * 4
    for base in range(0, 4 * PAD, CHUNK):
        at = slice(base, base + CHUNK)
        j, lo = base // PAD, base % PAD
        src, lo = (a_ref, base) if j < 2 else ((b0_ref, b1_ref)[j - 2], lo)
        normed, inverse = layer_norm(mid_ref[at, :])
        t = src[lo : lo + CHUNK, :].astype(F32)
        g = g_ref[at, :].astype(F32)
        d = g + norm_reverse(t * gain, normed, inverse)
        low_ref[at, :] = d.astype(BF16)
        if base < PAD:
            own_ref[at, :] = d
            new = [jnp.sum(v, axis=0, keepdims=True) for v in (t * normed, t, d, g)]
            sums = [c + n for c, n in zip(sums, new)]
    sum_ref[...] = jnp.concatenate(list(sums) + [jnp.zeros((4, D), F32)], axis=0)


def middle_back(image, mid, a, rest, g, small):
    rows = 4 * PAD
    full = lambda shape: pl.BlockSpec(shape, lambda i: (0, 0))
    part = pl.BlockSpec((rows, D), lambda i: (image, 0))
    return pl.pallas_call(
        middle_back_kernel,
        grid=(1,),
        in_specs=[part, full(a.shape), full((PAD, D)), full((PAD, D)), part, full(small.shape)],
        out_specs=[full((rows, D)), full((PAD, D)), full((8, D))],
        out_shape=[
            jax.ShapeDtypeStruct((rows, D), BF16),
            jax.ShapeDtypeStruct((PAD, D), F32),
            jax.ShapeDtypeStruct((8, D), F32),
        ],
        compiler_params=params(32),
        cost_estimate=cost(2.2),
        name="middle_back",
    )(mid, a, *rest, g, small)


def pieces_of(length):
    return [(lo, min(CHUNK, length - lo)) for lo in range(0, length, CHUNK)]


def result_kernel(n_img, *refs):
    mids, mine, got = refs[:n_img], refs[n_img : 2 * n_img], refs[2 * n_img : 3 * n_img]
    vec_ref, out_ref = refs[3 * n_img :]
    shift = vec_ref[7:8, :]
    for i in range(n_img):
        for lo, n in pieces_of(out_ref.shape[1]):
            at = slice(lo, lo + n)
            total = mids[i][at, :] + mine[i][at, :].astype(F32) + got[i][at, :].astype(F32)
            out_ref[i, at, :] = (total + shift).astype(BF16)


def result_rows(length, middle, mine, got, small):
    n_img = len(mine)
    spec = pl.BlockSpec((PAD, D), lambda i: (0, 0))
    own = [pl.BlockSpec((PAD, D), lambda i, k=k: (4 * k, 0)) for k in range(n_img)]
    return pl.pallas_call(
        functools.partial(result_kernel, n_img),
        grid=(1,),
        in_specs=own + [spec] * (2 * n_img) + [pl.BlockSpec(small.shape, lambda i: (0, 0))],
        out_specs=pl.BlockSpec((n_img, length, D), lambda i: (0, 0, 0)),
        out_shape=jax.ShapeDtypeStruct((n_img, length, D), BF16),
        compiler_params=params(32),
        cost_estimate=cost(1.5),
        name="result",
    )(*[middle] * n_img, *mine, *got, small)


def tokens_back_kernel(n_img, x_ref, *refs):
    dmid, mine, got = refs[:n_img], refs[n_img : 2 * n_img], refs[2 * n_img : 3 * n_img]
    vec_ref, out_ref, sum_ref = refs[3 * n_img :]
    gain = vec_ref[0:1, :]
    first = jnp.zeros((1, D), F32)
    second = jnp.zeros((1, D), F32)
    for i in range(n_img):
        for lo, n in pieces_of(out_ref.shape[1]):
            at = slice(lo, lo + n)
            normed, inverse = layer_norm(x_ref[i, at, :].astype(F32))
            u = mine[i][at, :].astype(F32) + got[i][at, :].astype(F32)
            first = first + jnp.sum(u * normed, axis=0, keepdims=True)
            second = second + jnp.sum(u, axis=0, keepdims=True)
            d = dmid[i][at, :] + norm_reverse(u * gain, normed, inverse)
            out_ref[i, at, :] = d.astype(BF16)
    sum_ref[...] = jnp.concatenate([first, second, jnp.zeros((6, D), F32)], axis=0)


def tokens_back(length, x, dmid, mine, got, small):
    n_img = len(dmid)
    spec = pl.BlockSpec((PAD, D), lambda i: (0, 0))
    return pl.pallas_call(
        functools.partial(tokens_back_kernel, n_img),
        grid=(1,),
        in_specs=[pl.BlockSpec(x.shape, lambda i: (0, 0, 0))]
        + [spec] * (3 * n_img)
        + [pl.BlockSpec(small.shape, lambda i: (0, 0))],
        out_specs=[
            pl.BlockSpec((n_img, length, D), lambda i: (0, 0, 0)),
            pl.BlockSpec((8, D), lambda i: (0, 0)),
        ],
        out_shape=[
            jax.ShapeDtypeStruct((n_img, length, D), BF16),
            jax.ShapeDtypeStruct((8, D), F32),
        ],
        compiler_params=params(32),
        cost_estimate=cost(2.0),
        name="tokens_back",
    )(x, *dmid, *mine, *got, small)


def pick_qkv_kernel(c_ref, w_ref, small_ref, out_ref):
    c = c_ref[0]
    rows = w_ref.shape[0]
    for p in range(2):
        for k in range(3):
            at = pl.multiple_of(k * D + c * 256 + p * 128, 128)
            to = p * 384 + k * 128
            out_ref[0:rows, to : to + 128] = w_ref[:, pl.ds(at, 128)]
    extra = small_ref.shape[0]
    out_ref[rows : rows + extra, 0:128] = small_ref[...]
    out_ref[rows : rows + extra, 128:768] = jnp.zeros((extra, 640), BF16)


def pick_qkv(c, weight, small):
    rows = weight.shape[0]
    smem = pl.BlockSpec(memory_space=pltpu.SMEM)
    vmem = pl.BlockSpec(memory_space=pltpu.VMEM)
    return pl.pallas_call(
        pick_qkv_kernel,
        in_specs=[smem, vmem, vmem],
        out_specs=vmem,
        out_shape=jax.ShapeDtypeStruct((rows + small.shape[0], 768), BF16),
        compiler_params=params(16),
        cost_estimate=cost(1.0),
        name="pick_qkv",
    )(c.astype(jnp.int32).reshape(1), weight, small)


def pick_fc1_kernel(wide, c_ref, w_ref, out_ref):
    c = c_ref[0]
    for k in range(out_ref.shape[1] // wide):
        at = pl.multiple_of(k * 4 * wide + c * wide, 128)
        out_ref[:, k * wide : (k + 1) * wide] = w_ref[:, pl.ds(at, wide)]


def pick_fc1(c, weight, wide):
    rows = weight.shape[0]
    if wide % 128:
        blocks = weight.reshape(rows, D // wide, 4, wide)
        return lax.dynamic_index_in_dim(blocks, c, 2, keepdims=False).reshape(rows, D)
    vmem = pl.BlockSpec(memory_space=pltpu.VMEM)
    return pl.pallas_call(
        functools.partial(pick_fc1_kernel, wide),
        in_specs=[pl.BlockSpec(memory_space=pltpu.SMEM), vmem],
        out_specs=vmem,
        out_shape=jax.ShapeDtypeStruct((rows, D), BF16),
        compiler_params=params(16),
        cost_estimate=cost(1.0),
        name="pick_fc1",
    )(c.astype(jnp.int32).reshape(1), weight)


def weave_kernel(bit_ref, a_ref, b_ref, o_ref):
    up = bit_ref[0]
    for i in range(a_ref.shape[0]):
        o_ref[i, up] = a_ref[i]
        o_ref[i, 1 - up] = b_ref[i]


def weave(bit, a, b):
    m, r, w = a.shape
    if r % 8 or w % 128:
        up = bit == 1
        low, high = jnp.where(up, b, a), jnp.where(up, a, b)
        return jnp.stack([low, high], axis=1)
    vmem = pl.BlockSpec(memory_space=pltpu.VMEM)
    out = pl.pallas_call(
        weave_kernel,
        in_specs=[pl.BlockSpec(memory_space=pltpu.SMEM), vmem, vmem],
        out_specs=vmem,
        out_shape=jax.ShapeDtypeStruct((m, 2, r, w), a.dtype),
        compiler_params=params(24),
        cost_estimate=cost(0.5 + m * r * w * 2e-6),
        name="weave",
    )(bit.astype(jnp.int32).reshape(1), a, b)
    return out


def weave_split_kernel(rows, bit_ref, a_ref, b_ref, w0_ref, w1_ref, small_ref):
    up = bit_ref[0]
    for i in range(a_ref.shape[0]):
        for src, which in ((a_ref, up), (b_ref, 1 - up)):
            w0_ref[i, which] = src[i, 0:rows, 0:384]
            w1_ref[i, which] = src[i, 0:rows, 384:768]
            at = pl.multiple_of((2 * i + which) * 128, 128)
            small_ref[:, pl.ds(at, 128)] = src[i, rows:, 0:128].astype(F32)


def weave_split(rows, bit, a, b):
    m, r, w = a.shape
    if 2 * m * 128 != D:
        both = weave(bit, a, b).reshape(2 * m, r, w)
        span = D // (2 * m)
        small = both[:, rows:, :span].transpose(1, 0, 2).reshape(r - rows, D)
        weights = both[:, :rows].reshape(-1, w)
        return [weights[:, :384], weights[:, 384:]], small.astype(F32)
    vmem = pl.BlockSpec(memory_space=pltpu.VMEM)
    w0, w1, small = pl.pallas_call(
        functools.partial(weave_split_kernel, rows),
        in_specs=[pl.BlockSpec(memory_space=pltpu.SMEM), vmem, vmem],
        out_specs=[vmem] * 3,
        out_shape=[jax.ShapeDtypeStruct((m, 2, rows, 384), a.dtype)] * 2
        + [jax.ShapeDtypeStruct((r - rows, D), F32)],
        compiler_params=params(24),
        cost_estimate=cost(1.0),
        name="weave_split",
    )(bit.astype(jnp.int32).reshape(1), a, b)
    return [w0.reshape(-1, 384), w1.reshape(-1, 384)], small


def place_qkv_kernel(c_ref, *refs):
    out_ref = refs[-1]
    c = c_ref[0]
    for slot, ref in enumerate(refs[:-1]):
        for pair in range(2):
            for k in range(3):
                at = pl.multiple_of(k * D + (c ^ SLOTS[slot]) * 256 + pair * 128, 128)
                src = pair * 384 + k * 128
                out_ref[:, pl.ds(at, 128)] = ref[:, src : src + 128].astype(F32)


def place_rest_kernel(r, wide, piece, c_ref, *refs):
    slots, (fc2_ref, fc1_ref, out_ref) = refs[:4], refs[4:]
    c = c_ref[0]
    for slot, ref in enumerate(slots):
        q = c ^ SLOTS[slot]
        fc2_ref[pl.ds(pl.multiple_of(q * wide, 8), wide), :] = ref[0:wide, :].astype(F32)
        for f in range(D // wide):
            at = pl.multiple_of(f * 4 * wide + q * wide, 128)
            fc1_ref[:, pl.ds(at, wide)] = ref[wide : wide + r, f * wide : (f + 1) * wide].astype(F32)
        out_ref[pl.ds(pl.multiple_of(q * piece, 8), piece), :] = ref[wide + r :, :].astype(F32)


def in_order(c, slots):
    own, y, core, both = slots
    odd = c % 2 == 1
    low = [jnp.where(odd, core, own), jnp.where(odd, own, core)]
    high = [jnp.where(odd, both, y), jnp.where(odd, y, both)]
    up = c // 2 == 1
    return jnp.stack(
        [jnp.where(up, b, a) for a, b in zip(low, high)]
        + [jnp.where(up, a, b) for a, b in zip(low, high)]
    )


def place_qkv(c, slots):
    r = slots[0].shape[0]
    smem = pl.BlockSpec(memory_space=pltpu.SMEM)
    vmem = pl.BlockSpec(memory_space=pltpu.VMEM)
    return pl.pallas_call(
        place_qkv_kernel,
        in_specs=[smem] + [vmem] * 4,
        out_specs=vmem,
        out_shape=jax.ShapeDtypeStruct((r, 3 * D), F32),
        compiler_params=params(24),
        cost_estimate=cost(1.5),
        name="place_qkv",
    )(c.astype(jnp.int32).reshape(1), *slots)


def place_rest(c, r, wide, piece, slots):
    if wide % 128 or piece % 8:
        full = in_order(c, slots).astype(F32)
        fc2 = full[:, :wide].reshape(-1, D)
        fc1 = full[:, wide : wide + r].reshape(4, r, D // wide, wide)
        fc1 = fc1.transpose(1, 2, 0, 3).reshape(r, 4 * D)
        return fc2, fc1, full[:, wide + r :].reshape(-1, D)
    smem = pl.BlockSpec(memory_space=pltpu.SMEM)
    vmem = pl.BlockSpec(memory_space=pltpu.VMEM)
    return pl.pallas_call(
        functools.partial(place_rest_kernel, r, wide, piece),
        in_specs=[smem] + [vmem] * 4,
        out_specs=[vmem] * 3,
        out_shape=[
            jax.ShapeDtypeStruct((4 * wide, D), F32),
            jax.ShapeDtypeStruct((r, 4 * D), F32),
            jax.ShapeDtypeStruct((4 * piece, D), F32),
        ],
        compiler_params=params(32),
        cost_estimate=cost(4.0),
        name="place_rest",
    )(c.astype(jnp.int32).reshape(1), *slots)


def gate(value, *after):
    flat = [v for a in after for v in (a if isinstance(a, (list, tuple)) else [a])]
    return lax.optimization_barrier((value, *flat))[0]


def body(
    nf,
    nc,
    tokens,
    out_grad,
    key_mask,
    slot_valid,
    norm_gains,
    norm_shifts,
    qkv_weight,
    qv_bias,
    out_weight,
    out_bias,
    fc1_weight,
    fc1_bias,
    fc2_weight,
    fc2_bias,
):
    f = lax.axis_index("fsdp")
    c = lax.axis_index("ctx")
    axes = ("fsdp", "ctx")
    bits = []
    while (1 << len(bits)) < nf:
        bits.append(1 << len(bits))

    def swap(v, df, dc):
        pairs = [(i * nc + j, (i ^ df) * nc + (j ^ dc)) for i in range(nf) for j in range(nc)]
        return lax.ppermute(v, axes, pairs)

    def core(v):
        return swap(v, 0, 1)

    def across(v):
        return swap(v, 0, 2)

    def flat(buf):
        return buf.reshape((-1,) + buf.shape[2:])

    class Doubling:
        def __init__(self, shard, split=0):
            self.buf, self.left, self.split, self.small = shard[None], list(reversed(bits)), split, None

        def step(self, token=None):
            b = self.left.pop(0)
            other = swap(self.buf, b, 0)
            if token is not None:
                other = gate(other, token)
            bit = (f // b) % 2
            if self.split and not self.left:
                self.buf, self.small = weave_split(self.split, bit, self.buf, other)
                return self.small
            out = weave(bit, self.buf, other)
            self.buf = out.reshape((-1,) + out.shape[2:])
            return out

        def all_but_last(self, token=None):
            while len(self.left) > 1:
                token = self.step(token)
            return token

    class Halving:
        def __init__(self, parts, low=BF16):
            self.parts, self.low, self.left = parts, low, list(bits)
            self.start()

        def start(self):
            b = self.left[0]
            up = (f // b) % 2
            send, self.keep = [], []
            for part in self.parts:
                v = part.reshape((part.shape[0] // 2, 2) + part.shape[1:])
                send.append(lax.dynamic_index_in_dim(v, 1 - up, 1, keepdims=False).astype(self.low))
                self.keep.append(lax.dynamic_index_in_dim(v, up, 1, keepdims=False))
            self.got = swap(jnp.concatenate(send, axis=-1), b, 0)

        def step(self, token=None):
            got = self.got if token is None else gate(self.got, token)
            at, parts = 0, []
            for keep in self.keep:
                parts.append(keep + got[..., at : at + keep.shape[-1]].astype(F32))
                at += keep.shape[-1]
            self.parts = parts
            self.left.pop(0)
            if self.left:
                self.start()
            return list(parts)

        def upto(self, count, token):
            while len(self.left) > count:
                token = self.step(token)
            return token

        def result(self):
            return jnp.concatenate([p[0] for p in self.parts], axis=-1)

    def slots_of(v):
        y = across(v)
        return [v, y, core(v), core(y)]

    n_img, length = tokens.shape[0], tokens.shape[1]
    images = range(n_img)
    quarter = D // nc
    rows_w = D // nf
    wide = 4 * D // nf // nc
    piece = rows_w // nc
    half = 2 * PAD

    mask_rows = jnp.pad(key_mask.astype(BF16), ((0, 0), (0, D - length)))[:, None, :]
    x_own = jnp.concatenate(
        [tokens, mask_rows, jnp.zeros((n_img, PAD - length - 1, D), BF16)], axis=1
    )
    x_slots = slots_of(x_own)

    small = jnp.concatenate(
        [
            norm_gains,
            norm_shifts,
            qv_bias,
            out_bias[None],
            fc2_bias[None],
            fc1_bias.reshape(4, D // nf),
        ],
        axis=0,
    )
    small = jnp.pad(small, ((0, 4), (0, 128 - D // nf)))
    qkv_w = Doubling(pick_qkv(c, qkv_weight, small), rows_w)

    out_pairs = []
    for fs in range(nf):
        for j in range(nc):
            dst_f = (fs % (nf // 4)) * 4 + j
            out_pairs.append((fs * nc + j, dst_f * nc + fs // (nf // 4)))
    out_back = [(b, a) for a, b in out_pairs]
    out_part = lax.dynamic_slice_in_dim(out_weight, c * piece, piece, 0)
    out_part = lax.ppermute(out_part, axes, out_pairs)
    token = qkv_w.step(out_part)
    out_w = Doubling(gate(out_part, token))
    while len(qkv_w.left) > 1:
        token = out_w.step(token)
        token = qkv_w.step(token)
    fc1_w = Doubling(gate(pick_fc1(c, fc1_weight, wide), token))
    token = out_w.all_but_last(token)
    fc2_part = lax.dynamic_slice_in_dim(fc2_weight, c * wide, wide, 0)

    position = c * length + jnp.arange(length)
    keep = (position < LIVE)[None, :] & (slot_valid[:, None] > 0)
    g_own = jnp.where(keep[:, :, None], out_grad, jnp.zeros((), BF16))
    g_own = jnp.pad(g_own, ((0, 0), (0, PAD - length), (0, 0)))
    g_slots = slots_of(gate(g_own, x_slots[1]))


    token = [fc1_w.step([token, x_slots[1]]), g_slots[1]]
    token = qkv_w.step(token)
    w_qkv, small = qkv_w.buf, qkv_w.small
    fc1_shift = lax.dynamic_slice_in_dim(small, 8 + c, 1, 0)
    qkv_shift = []
    for p in range(2):
        q_shift = lax.dynamic_slice(small, (4, c * quarter + p * 128), (1, 128))
        v_shift = lax.dynamic_slice(small, (5, c * quarter + p * 128), (1, 128))
        qkv_shift.append(jnp.concatenate([q_shift, jnp.zeros_like(q_shift), v_shift], axis=1))

    def rows_of(v, i, first=0, count=4):
        return v[(4 * i + first) * PAD : (4 * i + first + count) * PAD]

    def send_rows(left, weight, i, product=dot):
        return product(rows_of(left, i, 2, 2), weight).astype(BF16)

    def mine_rows(left, weight, i, got, product=dot):
        return (product(rows_of(left, i, 0, 2), weight) + got.astype(F32)).astype(BF16)

    def total_of(mine, got):
        got = jnp.concatenate([got[PAD:], got[:PAD]], axis=0)
        return (mine.astype(F32) + got.astype(F32)).astype(BF16)

    def core_halves(v):
        return [core(v[:PAD]), core(v[PAD:])]

    normed, bias = prepare([gate(x_slots[0], token)] + x_slots[1:], small)
    qkv, lse, contexts = [], [], []
    for p in range(2):
        qkv.append((dot(normed, w_qkv[p]) + qkv_shift[p]).astype(BF16))
        out = attention(n_img, gate(qkv[p], token), bias)
        contexts.append(out[0])
        lse.append(out[1])
        token = out[0]
        if p == 0:
            token = fc1_w.all_but_last(token)
            fc2_w = Doubling(gate(fc2_part, token))
    token = out_w.step(token)
    w_out = flat(out_w.buf)
    context = jnp.concatenate(contexts, axis=1)
    sends = [send_rows(gate(context, token), w_out, i) for i in images]
    mine1, got1 = [], []
    for i in images:
        mine1.append(mine_rows(context, w_out, i, core(sends[i])))
        got1.append(across(mine1[i]))
    token = fc2_w.step(mine1[-1])
    g_all = stack_rows(g_slots)

    parts = []
    for i in images:
        if i == n_img - 1:
            token = fc1_w.step(token)
            w_fc1 = flat(fc1_w.buf)
            token = fc2_w.all_but_last(token)
        got = gate(got1[i], token)
        total = total_of(mine1[i], got)
        parts += [mine1[i], got] + core_halves(total)
        token = total
    middle, normed_mid = middle_rows(x_slots, [gate(parts[0], token)] + parts[1:], small)
    pre = dot(normed_mid, w_fc1) + fc1_shift
    sig = jax.nn.sigmoid(1.702 * pre)
    hidden = (pre * sig).astype(BF16)
    p_fc2 = dot_tn(hidden, g_all)
    token = fc2_w.step(p_fc2)
    w_fc2 = flat(fc2_w.buf)
    fc2_g = Halving([gate(p_fc2, token).reshape(nf, -1, D)])

    d_hidden = dot_nt(g_all, w_fc2)
    d_pre = d_hidden * (sig + 1.702 * pre * sig * (1.0 - sig))
    fc1_sum = jnp.sum(d_pre, axis=0, keepdims=True)
    d_pre_low = d_pre.astype(BF16)
    sends = [send_rows(d_pre_low, w_fc1, i, dot_nt) for i in images]
    mine2, got2 = [], []
    for i in images:
        mine2.append(mine_rows(d_pre_low, w_fc1, i, core(sends[i]), dot_nt))
        got2.append(across(gate(mine2[i], *got2)))
    p_fc1 = dot_tn(gate(normed_mid, mine2[-1]), d_pre_low)
    token = p_fc1

    d_mid_low, d_mid_own, mid_sums, d_context = [], [], [], []
    d_raw = [[None] * n_img for _ in range(2)]
    qv_sum, mine3, got3 = [], [], []

    def back_rows(i, token):
        parts = [d_raw[0][i], gate(d_raw[1][i], token)]
        send = sum(dot_nt(parts[p][half:], w_qkv[p]) for p in range(2)).astype(BF16)
        mine = sum(dot_nt(parts[p][:half], w_qkv[p]) for p in range(2))
        mine = (mine + core(send).astype(F32)).astype(BF16)
        mine3.append(mine)
        got3.append(across(gate(mine[PAD:], *got2, *got3)))
        return mine

    for i in images:
        token = total = total_of(mine2[i], gate(got2[i], token))
        if i == 0:
            token = fc2_g.step(token)
            fc1_g = Halving([gate(p_fc1, token).reshape(nf, -1, D)])
        low, own, sums = middle_back(i, middle, gate(total, token), core_halves(total), g_all, small)
        d_mid_low.append(low)
        d_mid_own.append(own)
        mid_sums.append(sums)
        d_context.append(dot_nt(low, w_out).astype(BF16))
        token = low
        if i == n_img - 1:
            p_out = sum(dot_tn(rows_of(context, k), d_mid_low[k]) for k in images)
            out_g = Halving([p_out.reshape(nf, -1, D)])
        sums = []
        for p in range(2):
            d_raw[p][i], s = attention_back(p, i, qkv[p], gate(d_context[i], token), bias, lse[p])
            token = d_raw[p][i]
            sums.append(s)
        qv_sum.append(sums)
        if i < n_img - 1:
            token = back_rows(i, token)
            token = fc2_g.step(token)

    p_qkv = [
        sum(dot_tn(rows_of(normed, k), gate(d_raw[p][k], token)) for k in images).reshape(nf, -1, 384)
        for p in range(2)
    ]
    token = [fc1_g.step(p_qkv)]
    qkv_g = Halving([gate(v, token) for v in p_qkv])
    token = back_rows(n_img - 1, token)
    token = fc2_g.upto(0, token)
    token = out_g.step(token)

    mines, gots = [], []
    sends = [send_rows(gate(hidden, token), w_fc2, i) for i in images]
    for i in images:
        mines.append(mine_rows(hidden, w_fc2, i, core(sends[i])))
        gots.append(across(gate(mines[i][PAD:], got3[-1])))
    token = fc1_g.step(mines[-1]) if fc1_g.left else mines[-1]
    token = out_g.step(token) if out_g.left else token
    token_gradient, tok_sums = tokens_back(length, gate(x_own, token), d_mid_own, mine3, got3, small)
    token = tok_sums

    mid_sum = sum(mid_sums[1:], mid_sums[0])
    fc1_rows = jnp.where((jnp.arange(4) == c)[:, None], fc1_sum, 0.0)
    here = (jnp.arange(D) // quarter == c)[None]
    qv_rows = [sum(s[p] for s in qv_sum[1:]) + qv_sum[0][p] for p in range(2)]
    qv_rows = jnp.concatenate([s[0:2] for s in qv_rows], axis=1)
    qv_rows = jnp.where(here, jnp.tile(qv_rows, (1, nc)), 0.0)
    packed = jnp.concatenate(
        [tok_sums[0:1], mid_sum[0:1], tok_sums[1:2], mid_sum[1:2], qv_rows, mid_sum[2:4], fc1_rows],
        axis=0,
    )
    vectors = Halving([packed.reshape(12, nf, D // nf).transpose(1, 0, 2)], F32)
    token = qkv_g.step(token)
    token = out_g.upto(0, token)
    out_part = lax.ppermute(out_g.result().astype(BF16), axes, out_back)
    token = vectors.step(token)
    token = fc1_g.upto(0, token)
    token = qkv_g.upto(1, token)
    token = vectors.upto(1, token)
    rest = [v.result().astype(BF16) for v in (fc2_g, fc1_g)]
    rest = jnp.concatenate(rest + [gate(out_part, token)], axis=0)
    rest_slots = slots_of(rest)
    token = qkv_g.upto(0, token)
    qkv_slots = slots_of(qkv_g.result().astype(BF16))
    vectors.upto(0, token)
    packed = vectors.result()
    packed = packed + across(packed)
    packed = packed + core(packed)

    result = result_rows(length, middle, mines, gots, small)
    qkv_full = place_qkv(c, qkv_slots)
    fc2_full, fc1_full, out_full = place_rest(c, rows_w, wide, piece, rest_slots)

    return (
        result,
        token_gradient,
        packed[0:2],
        packed[2:4],
        qkv_full,
        packed[4:6],
        out_full,
        packed[6],
        fc1_full,
        packed[8:12].reshape(-1),
        fc2_full,
        packed[7],
    )


def solution(mesh):
    in_specs = (
        P("fsdp", "ctx", None),
        P("fsdp", "ctx", None),
        P("fsdp", "ctx"),
        P("fsdp"),
        P(None, "fsdp"),
        P(None, "fsdp"),
        P("fsdp", None),
        P(None, "fsdp"),
        P("fsdp", None),
        P("fsdp"),
        P("fsdp", None),
        P("fsdp"),
        P("fsdp", None),
        P("fsdp"),
    )
    out_specs = (
        P("fsdp", "ctx", None),
        P("fsdp", "ctx", None),
        P(None, "fsdp"),
        P(None, "fsdp"),
        P("fsdp", None),
        P(None, "fsdp"),
        P("fsdp", None),
        P("fsdp"),
        P("fsdp", None),
        P("fsdp"),
        P("fsdp", None),
        P("fsdp"),
    )
    step = functools.partial(body, mesh.shape["fsdp"], mesh.shape["ctx"])
    return jax.shard_map(step, mesh=mesh, in_specs=in_specs, out_specs=out_specs, check_vma=False)
```

```python
import functools

import jax
import jax.numpy as jnp
from jax import lax
from jax.experimental import pallas as pl
from jax.experimental.pallas import tpu as pltpu
from jax.sharding import PartitionSpec as P

D = 1024
HEADS = 16
HEAD_DIM = 64
LIVE = 577
PAD = 160
MASK_ROW = 148
NEG = -1e30
F32 = jnp.float32
BF16 = jnp.bfloat16


def dot(a, b):
    return lax.dot_general(a, b, (((1,), (0,)), ((), ())), preferred_element_type=F32)


def dot_nt(a, b):
    return lax.dot_general(a, b, (((1,), (1,)), ((), ())), preferred_element_type=F32)


def dot_tn(a, b):
    return lax.dot_general(a, b, (((0,), (0,)), ((), ())), preferred_element_type=F32)


def layer_norm(values):
    centred = values - jnp.mean(values, axis=-1, keepdims=True)
    inverse = lax.rsqrt(jnp.mean(centred * centred, axis=-1, keepdims=True) + 1e-05)
    return centred * inverse, inverse


def norm_reverse(grad, normed, inverse):
    first = jnp.mean(grad, axis=-1, keepdims=True)
    second = jnp.mean(grad * normed, axis=-1, keepdims=True)
    return inverse * (grad - first - normed * second)


def attn_fwd_kernel(qkv_ref, bias_ref, o_ref, lse_ref):
    lane = lax.broadcasted_iota(jnp.int32, (1, 128), 1)
    q = qkv_ref[:, 0:128] * 0.125
    k = qkv_ref[:, 128:256]
    v = qkv_ref[:, 256:384]
    bias = bias_ref[:, 0:1]
    outs = []
    lse_ref[2:8, :] = jnp.zeros((6, lse_ref.shape[1]), F32)
    for h in range(2):
        qh = jnp.where((lane // 64) == h, q, jnp.zeros_like(q))
        s = dot_nt(k, qh) + bias
        top = jnp.max(s, axis=0, keepdims=True)
        e = jnp.exp(s - top)
        total = jnp.sum(e, axis=0, keepdims=True)
        p = (e * (1.0 / total)).astype(BF16)
        lse_ref[h : h + 1, :] = top + jnp.log(total)
        outs.append(dot_tn(p, v))
    o_ref[...] = jnp.where(lane < 64, outs[0], outs[1]).astype(BF16)


def attn_bwd_kernel(qkv_ref, g_ref, bias_ref, lse_ref, d_ref, sum_ref, dq_acc, dk_acc, dv_acc):
    lane = lax.broadcasted_iota(jnp.int32, (1, 128), 1)
    dk_acc[...] = jnp.zeros_like(dk_acc)
    dv_acc[...] = jnp.zeros_like(dv_acc)

    def head(h, carry):
        q = qkv_ref[:, 0:128] * 0.125
        k = qkv_ref[:, 128:256]
        v = qkv_ref[:, 256:384]
        g = g_ref[...]
        mine = (lane // 64) == h
        qh = jnp.where(mine, q, jnp.zeros_like(q))
        gh = jnp.where(mine, g, jnp.zeros_like(g))
        s = dot_nt(k, qh) + bias_ref[:, 0:1]
        p = jnp.exp(s - lse_ref[pl.ds(h, 1), :])
        dp = dot_nt(v, gh)
        delta = jnp.sum(p * dp, axis=0, keepdims=True)
        ds = (p * (dp - delta)).astype(BF16)
        dv_acc[...] += dot(p.astype(BF16), gh)
        dk_acc[...] += dot(ds, qh)
        dq_acc[...] = jnp.where(mine, dot_tn(ds, k) * 0.125, dq_acc[...])
        return carry

    lax.fori_loop(0, 2, head, 0)
    dq = dq_acc[...]
    dv = dv_acc[...]
    d_ref[:, 0:128] = dq.astype(BF16)
    d_ref[:, 128:256] = dk_acc[...].astype(BF16)
    d_ref[:, 256:384] = dv.astype(BF16)
    sums = [jnp.sum(x, axis=0, keepdims=True) for x in (dq, dv)]
    sum_ref[...] = jnp.concatenate(sums + [jnp.zeros((6, 128), F32)], axis=0)


def params(mib):
    return pltpu.CompilerParams(vmem_limit_bytes=mib << 20)


def cost(us):
    return pl.CostEstimate(flops=int(us * 1e7), bytes_accessed=1024, transcendentals=0)


def attention(n_img, qkv, bias_col):
    rows = qkv.shape[0] // n_img
    spec = lambda w: pl.BlockSpec((rows, w), lambda i: (i, 0))
    return pl.pallas_call(
        attn_fwd_kernel,
        grid=(n_img,),
        in_specs=[spec(384), spec(128)],
        out_specs=[spec(128), pl.BlockSpec((8, rows), lambda i: (i, 0))],
        out_shape=[
            jax.ShapeDtypeStruct((n_img * rows, 128), BF16),
            jax.ShapeDtypeStruct((n_img * 8, rows), F32),
        ],
        compiler_params=params(48),
        cost_estimate=cost(4.0),
        name="attn_fwd",
    )(qkv, bias_col)


def attention_back(pair, image, qkv, grad, bias_col, lse):
    rows = grad.shape[0]
    full = lambda shape: pl.BlockSpec(shape, lambda i: (0, 0))
    return pl.pallas_call(
        attn_bwd_kernel,
        grid=(1,),
        in_specs=[
            pl.BlockSpec((rows, 384), lambda i: (image, 0)),
            pl.BlockSpec((rows, 128), lambda i: (0, pair)),
            pl.BlockSpec((rows, 128), lambda i: (image, 0)),
            pl.BlockSpec((8, rows), lambda i: (image, 0)),
        ],
        out_specs=[full((rows, 384)), full((8, 128))],
        out_shape=[
            jax.ShapeDtypeStruct((rows, 384), BF16),
            jax.ShapeDtypeStruct((8, 128), F32),
        ],
        scratch_shapes=[pltpu.VMEM((rows, 128), F32)] * 3,
        compiler_params=params(48),
        cost_estimate=cost(3.7),
        name="attn_bwd",
    )(qkv, grad, bias_col, lse)


CHUNK = 32
SLOTS = (0, 2, 1, 3)


def prepare_kernel(n_img, *refs):
    slots, (vec_ref, out_ref, bias_ref) = refs[:4], refs[4:]
    gain, add = vec_ref[0:1, :], vec_ref[2:3, :]
    row = lax.broadcasted_iota(jnp.int32, (PAD, PAD), 0)
    lane = lax.broadcasted_iota(jnp.int32, (PAD, PAD), 1)

    def image(i, carry):
        for j, src in enumerate(slots):
            base = pl.multiple_of(i * 4 * PAD + j * PAD, PAD)
            for lo in range(0, PAD, CHUNK):
                normed, _ = layer_norm(src[i, lo : lo + CHUNK, :].astype(F32))
                out_ref[pl.ds(base + lo, CHUNK), :] = (normed * gain + add).astype(BF16)
            mask = src[i, MASK_ROW : MASK_ROW + 1, 0:PAD].astype(F32)
            hidden = jnp.where(row == lane, (1.0 - mask) * NEG, 0.0)
            hidden = jnp.sum(hidden, axis=1, keepdims=True)
            bias_ref[pl.ds(base, PAD), :] = jnp.broadcast_to(hidden, (PAD, 128))
        return carry

    lax.fori_loop(0, n_img, image, 0)


def prepare(slots, small):
    n_img = slots[0].shape[0]
    rows = n_img * 4 * PAD
    return pl.pallas_call(
        functools.partial(prepare_kernel, n_img),
        out_shape=[
            jax.ShapeDtypeStruct((rows, D), BF16),
            jax.ShapeDtypeStruct((rows, 128), F32),
        ],
        compiler_params=params(40),
        cost_estimate=cost(4.2),
        name="prepare",
    )(*slots, small)


def stack_kernel(n_img, *refs):
    slots, out_ref = refs[:4], refs[4]
    for i in range(n_img):
        for j, src in enumerate(slots):
            base = (4 * i + j) * PAD
            out_ref[base : base + PAD, :] = src[i]


def stack_rows(slots):
    n_img = slots[0].shape[0]
    return pl.pallas_call(
        functools.partial(stack_kernel, n_img),
        out_shape=jax.ShapeDtypeStruct((n_img * 4 * PAD, D), BF16),
        compiler_params=params(32),
        cost_estimate=cost(2.0),
        name="stack_rows",
    )(*slots)


def middle_kernel(n_img, *refs):
    slots, parts = refs[:4], refs[4 : 4 + 4 * n_img]
    vec_ref, mid_ref, out_ref = refs[4 + 4 * n_img :]
    shift, gain, add = vec_ref[6:7, :], vec_ref[1:2, :], vec_ref[3:4, :]
    for i in range(n_img):
        mine, got = parts[4 * i], parts[4 * i + 1]
        rest = parts[4 * i + 2 : 4 * i + 4]
        for j, src in enumerate(slots):
            for lo in range(0, PAD, CHUNK):
                near = slice(lo, lo + CHUNK)
                if j < 2:
                    far = slice((1 - j) * PAD + lo, (1 - j) * PAD + lo + CHUNK)
                    own = slice(j * PAD + lo, j * PAD + lo + CHUNK)
                    part = mine[own, :].astype(F32) + got[far, :].astype(F32)
                    part = part.astype(BF16).astype(F32)
                else:
                    part = rest[j - 2][near, :].astype(F32)
                at = slice((4 * i + j) * PAD + lo, (4 * i + j) * PAD + lo + CHUNK)
                m = src[i, near, :].astype(F32) + shift + part
                mid_ref[at, :] = m
                normed, _ = layer_norm(m)
                out_ref[at, :] = (normed * gain + add).astype(BF16)


def middle_rows(slots, parts, small):
    n_img = slots[0].shape[0]
    rows = n_img * 4 * PAD
    return pl.pallas_call(
        functools.partial(middle_kernel, n_img),
        out_shape=[
            jax.ShapeDtypeStruct((rows, D), F32),
            jax.ShapeDtypeStruct((rows, D), BF16),
        ],
        compiler_params=params(40),
        cost_estimate=cost(5.0),
        name="middle",
    )(*slots, *parts, small)


def middle_back_kernel(mid_ref, a_ref, b0_ref, b1_ref, g_ref, vec_ref, low_ref, own_ref, sum_ref):
    gain = vec_ref[1:2, :]
    sums = [jnp.zeros((1, D), F32)] * 4
    for base in range(0, 4 * PAD, CHUNK):
        at = slice(base, base + CHUNK)
        j, lo = base // PAD, base % PAD
        src, lo = (a_ref, base) if j < 2 else ((b0_ref, b1_ref)[j - 2], lo)
        normed, inverse = layer_norm(mid_ref[at, :])
        t = src[lo : lo + CHUNK, :].astype(F32)
        g = g_ref[at, :].astype(F32)
        d = g + norm_reverse(t * gain, normed, inverse)
        low_ref[at, :] = d.astype(BF16)
        if base < PAD:
            own_ref[at, :] = d
            new = [jnp.sum(v, axis=0, keepdims=True) for v in (t * normed, t, d, g)]
            sums = [c + n for c, n in zip(sums, new)]
    sum_ref[...] = jnp.concatenate(list(sums) + [jnp.zeros((4, D), F32)], axis=0)


def middle_back(image, mid, a, rest, g, small):
    rows = 4 * PAD
    full = lambda shape: pl.BlockSpec(shape, lambda i: (0, 0))
    part = pl.BlockSpec((rows, D), lambda i: (image, 0))
    return pl.pallas_call(
        middle_back_kernel,
        grid=(1,),
        in_specs=[part, full(a.shape), full((PAD, D)), full((PAD, D)), part, full(small.shape)],
        out_specs=[full((rows, D)), full((PAD, D)), full((8, D))],
        out_shape=[
            jax.ShapeDtypeStruct((rows, D), BF16),
            jax.ShapeDtypeStruct((PAD, D), F32),
            jax.ShapeDtypeStruct((8, D), F32),
        ],
        compiler_params=params(32),
        cost_estimate=cost(2.2),
        name="middle_back",
    )(mid, a, *rest, g, small)


def pieces_of(length):
    return [(lo, min(CHUNK, length - lo)) for lo in range(0, length, CHUNK)]


def result_kernel(n_img, *refs):
    mids, mine, got = refs[:n_img], refs[n_img : 2 * n_img], refs[2 * n_img : 3 * n_img]
    vec_ref, out_ref = refs[3 * n_img :]
    shift = vec_ref[7:8, :]
    for i in range(n_img):
        for lo, n in pieces_of(out_ref.shape[1]):
            at = slice(lo, lo + n)
            total = mids[i][at, :] + mine[i][at, :].astype(F32) + got[i][at, :].astype(F32)
            out_ref[i, at, :] = (total + shift).astype(BF16)


def result_rows(length, middle, mine, got, small):
    n_img = len(mine)
    spec = pl.BlockSpec((PAD, D), lambda i: (0, 0))
    own = [pl.BlockSpec((PAD, D), lambda i, k=k: (4 * k, 0)) for k in range(n_img)]
    return pl.pallas_call(
        functools.partial(result_kernel, n_img),
        grid=(1,),
        in_specs=own + [spec] * (2 * n_img) + [pl.BlockSpec(small.shape, lambda i: (0, 0))],
        out_specs=pl.BlockSpec((n_img, length, D), lambda i: (0, 0, 0)),
        out_shape=jax.ShapeDtypeStruct((n_img, length, D), BF16),
        compiler_params=params(32),
        cost_estimate=cost(1.5),
        name="result",
    )(*[middle] * n_img, *mine, *got, small)


def tokens_back_kernel(n_img, x_ref, *refs):
    dmid, mine, got = refs[:n_img], refs[n_img : 2 * n_img], refs[2 * n_img : 3 * n_img]
    vec_ref, out_ref, sum_ref = refs[3 * n_img :]
    gain = vec_ref[0:1, :]
    first = jnp.zeros((1, D), F32)
    second = jnp.zeros((1, D), F32)
    for i in range(n_img):
        for lo, n in pieces_of(out_ref.shape[1]):
            at = slice(lo, lo + n)
            normed, inverse = layer_norm(x_ref[i, at, :].astype(F32))
            u = mine[i][at, :].astype(F32) + got[i][at, :].astype(F32)
            first = first + jnp.sum(u * normed, axis=0, keepdims=True)
            second = second + jnp.sum(u, axis=0, keepdims=True)
            d = dmid[i][at, :] + norm_reverse(u * gain, normed, inverse)
            out_ref[i, at, :] = d.astype(BF16)
    sum_ref[...] = jnp.concatenate([first, second, jnp.zeros((6, D), F32)], axis=0)


def tokens_back(length, x, dmid, mine, got, small):
    n_img = len(dmid)
    spec = pl.BlockSpec((PAD, D), lambda i: (0, 0))
    return pl.pallas_call(
        functools.partial(tokens_back_kernel, n_img),
        grid=(1,),
        in_specs=[pl.BlockSpec(x.shape, lambda i: (0, 0, 0))]
        + [spec] * (3 * n_img)
        + [pl.BlockSpec(small.shape, lambda i: (0, 0))],
        out_specs=[
            pl.BlockSpec((n_img, length, D), lambda i: (0, 0, 0)),
            pl.BlockSpec((8, D), lambda i: (0, 0)),
        ],
        out_shape=[
            jax.ShapeDtypeStruct((n_img, length, D), BF16),
            jax.ShapeDtypeStruct((8, D), F32),
        ],
        compiler_params=params(32),
        cost_estimate=cost(2.0),
        name="tokens_back",
    )(x, *dmid, *mine, *got, small)


def pick_qkv_kernel(c_ref, w_ref, small_ref, out_ref):
    c = c_ref[0]
    rows = w_ref.shape[0]
    for p in range(2):
        for k in range(3):
            at = pl.multiple_of(k * D + c * 256 + p * 128, 128)
            to = p * 384 + k * 128
            out_ref[0:rows, to : to + 128] = w_ref[:, pl.ds(at, 128)]
    extra = small_ref.shape[0]
    out_ref[rows : rows + extra, 0:128] = small_ref[...]
    out_ref[rows : rows + extra, 128:768] = jnp.zeros((extra, 640), BF16)


def pick_qkv(c, weight, small):
    rows = weight.shape[0]
    smem = pl.BlockSpec(memory_space=pltpu.SMEM)
    vmem = pl.BlockSpec(memory_space=pltpu.VMEM)
    return pl.pallas_call(
        pick_qkv_kernel,
        in_specs=[smem, vmem, vmem],
        out_specs=vmem,
        out_shape=jax.ShapeDtypeStruct((rows + small.shape[0], 768), BF16),
        compiler_params=params(16),
        cost_estimate=cost(1.0),
        name="pick_qkv",
    )(c.astype(jnp.int32).reshape(1), weight, small)


def pick_fc1_kernel(wide, c_ref, w_ref, out_ref):
    c = c_ref[0]
    for k in range(out_ref.shape[1] // wide):
        at = pl.multiple_of(k * 4 * wide + c * wide, 128)
        out_ref[:, k * wide : (k + 1) * wide] = w_ref[:, pl.ds(at, wide)]


def pick_fc1(c, weight, wide):
    rows = weight.shape[0]
    if wide % 128:
        blocks = weight.reshape(rows, D // wide, 4, wide)
        return lax.dynamic_index_in_dim(blocks, c, 2, keepdims=False).reshape(rows, D)
    vmem = pl.BlockSpec(memory_space=pltpu.VMEM)
    return pl.pallas_call(
        functools.partial(pick_fc1_kernel, wide),
        in_specs=[pl.BlockSpec(memory_space=pltpu.SMEM), vmem],
        out_specs=vmem,
        out_shape=jax.ShapeDtypeStruct((rows, D), BF16),
        compiler_params=params(16),
        cost_estimate=cost(1.0),
        name="pick_fc1",
    )(c.astype(jnp.int32).reshape(1), weight)


def weave_kernel(bit_ref, a_ref, b_ref, o_ref):
    up = bit_ref[0]
    for i in range(a_ref.shape[0]):
        o_ref[i, up] = a_ref[i]
        o_ref[i, 1 - up] = b_ref[i]


def weave(bit, a, b):
    m, r, w = a.shape
    if r % 8 or w % 128:
        up = bit == 1
        low, high = jnp.where(up, b, a), jnp.where(up, a, b)
        return jnp.stack([low, high], axis=1)
    vmem = pl.BlockSpec(memory_space=pltpu.VMEM)
    out = pl.pallas_call(
        weave_kernel,
        in_specs=[pl.BlockSpec(memory_space=pltpu.SMEM), vmem, vmem],
        out_specs=vmem,
        out_shape=jax.ShapeDtypeStruct((m, 2, r, w), a.dtype),
        compiler_params=params(24),
        cost_estimate=cost(0.5 + m * r * w * 2e-6),
        name="weave",
    )(bit.astype(jnp.int32).reshape(1), a, b)
    return out


def weave_split_kernel(rows, bit_ref, a_ref, b_ref, w0_ref, w1_ref, small_ref):
    up = bit_ref[0]
    for i in range(a_ref.shape[0]):
        for src, which in ((a_ref, up), (b_ref, 1 - up)):
            w0_ref[i, which] = src[i, 0:rows, 0:384]
            w1_ref[i, which] = src[i, 0:rows, 384:768]
            at = pl.multiple_of((2 * i + which) * 128, 128)
            small_ref[:, pl.ds(at, 128)] = src[i, rows:, 0:128].astype(F32)


def weave_split(rows, bit, a, b):
    m, r, w = a.shape
    if 2 * m * 128 != D:
        both = weave(bit, a, b).reshape(2 * m, r, w)
        span = D // (2 * m)
        small = both[:, rows:, :span].transpose(1, 0, 2).reshape(r - rows, D)
        weights = both[:, :rows].reshape(-1, w)
        return [weights[:, :384], weights[:, 384:]], small.astype(F32)
    vmem = pl.BlockSpec(memory_space=pltpu.VMEM)
    w0, w1, small = pl.pallas_call(
        functools.partial(weave_split_kernel, rows),
        in_specs=[pl.BlockSpec(memory_space=pltpu.SMEM), vmem, vmem],
        out_specs=[vmem] * 3,
        out_shape=[jax.ShapeDtypeStruct((m, 2, rows, 384), a.dtype)] * 2
        + [jax.ShapeDtypeStruct((r - rows, D), F32)],
        compiler_params=params(24),
        cost_estimate=cost(1.0),
        name="weave_split",
    )(bit.astype(jnp.int32).reshape(1), a, b)
    return [w0.reshape(-1, 384), w1.reshape(-1, 384)], small


def place_qkv_kernel(c_ref, *refs):
    out_ref = refs[-1]
    c = c_ref[0]
    for slot, ref in enumerate(refs[:-1]):
        for pair in range(2):
            for k in range(3):
                at = pl.multiple_of(k * D + (c ^ SLOTS[slot]) * 256 + pair * 128, 128)
                src = pair * 384 + k * 128
                out_ref[:, pl.ds(at, 128)] = ref[:, src : src + 128].astype(F32)


def place_rest_kernel(r, wide, piece, c_ref, *refs):
    slots, (fc2_ref, fc1_ref, out_ref) = refs[:4], refs[4:]
    c = c_ref[0]
    for slot, ref in enumerate(slots):
        q = c ^ SLOTS[slot]
        fc2_ref[pl.ds(pl.multiple_of(q * wide, 8), wide), :] = ref[0:wide, :].astype(F32)
        for f in range(D // wide):
            at = pl.multiple_of(f * 4 * wide + q * wide, 128)
            fc1_ref[:, pl.ds(at, wide)] = ref[wide : wide + r, f * wide : (f + 1) * wide].astype(F32)
        out_ref[pl.ds(pl.multiple_of(q * piece, 8), piece), :] = ref[wide + r :, :].astype(F32)


def in_order(c, slots):
    own, y, core, both = slots
    odd = c % 2 == 1
    low = [jnp.where(odd, core, own), jnp.where(odd, own, core)]
    high = [jnp.where(odd, both, y), jnp.where(odd, y, both)]
    up = c // 2 == 1
    return jnp.stack(
        [jnp.where(up, b, a) for a, b in zip(low, high)]
        + [jnp.where(up, a, b) for a, b in zip(low, high)]
    )


def place_qkv(c, slots):
    r = slots[0].shape[0]
    smem = pl.BlockSpec(memory_space=pltpu.SMEM)
    vmem = pl.BlockSpec(memory_space=pltpu.VMEM)
    return pl.pallas_call(
        place_qkv_kernel,
        in_specs=[smem] + [vmem] * 4,
        out_specs=vmem,
        out_shape=jax.ShapeDtypeStruct((r, 3 * D), F32),
        compiler_params=params(24),
        cost_estimate=cost(1.5),
        name="place_qkv",
    )(c.astype(jnp.int32).reshape(1), *slots)


def place_rest(c, r, wide, piece, slots):
    if wide % 128 or piece % 8:
        full = in_order(c, slots).astype(F32)
        fc2 = full[:, :wide].reshape(-1, D)
        fc1 = full[:, wide : wide + r].reshape(4, r, D // wide, wide)
        fc1 = fc1.transpose(1, 2, 0, 3).reshape(r, 4 * D)
        return fc2, fc1, full[:, wide + r :].reshape(-1, D)
    smem = pl.BlockSpec(memory_space=pltpu.SMEM)
    vmem = pl.BlockSpec(memory_space=pltpu.VMEM)
    return pl.pallas_call(
        functools.partial(place_rest_kernel, r, wide, piece),
        in_specs=[smem] + [vmem] * 4,
        out_specs=[vmem] * 3,
        out_shape=[
            jax.ShapeDtypeStruct((4 * wide, D), F32),
            jax.ShapeDtypeStruct((r, 4 * D), F32),
            jax.ShapeDtypeStruct((4 * piece, D), F32),
        ],
        compiler_params=params(32),
        cost_estimate=cost(4.0),
        name="place_rest",
    )(c.astype(jnp.int32).reshape(1), *slots)


def gate(value, *after):
    flat = [v for a in after for v in (a if isinstance(a, (list, tuple)) else [a])]
    return lax.optimization_barrier((value, *flat))[0]


def body(
    nf,
    nc,
    tokens,
    out_grad,
    key_mask,
    slot_valid,
    norm_gains,
    norm_shifts,
    qkv_weight,
    qv_bias,
    out_weight,
    out_bias,
    fc1_weight,
    fc1_bias,
    fc2_weight,
    fc2_bias,
):
    f = lax.axis_index("fsdp")
    c = lax.axis_index("ctx")
    axes = ("fsdp", "ctx")
    bits = []
    while (1 << len(bits)) < nf:
        bits.append(1 << len(bits))

    def swap(v, df, dc):
        pairs = [(i * nc + j, (i ^ df) * nc + (j ^ dc)) for i in range(nf) for j in range(nc)]
        return lax.ppermute(v, axes, pairs)

    def core(v):
        return swap(v, 0, 1)

    def across(v):
        return swap(v, 0, 2)

    def flat(buf):
        return buf.reshape((-1,) + buf.shape[2:])

    class Doubling:
        def __init__(self, shard, split=0):
            self.buf, self.left, self.split, self.small = shard[None], list(reversed(bits)), split, None

        def step(self, token=None):
            b = self.left.pop(0)
            other = swap(self.buf, b, 0)
            if token is not None:
                other = gate(other, token)
            bit = (f // b) % 2
            if self.split and not self.left:
                self.buf, self.small = weave_split(self.split, bit, self.buf, other)
                return self.small
            out = weave(bit, self.buf, other)
            self.buf = out.reshape((-1,) + out.shape[2:])
            return out

        def all_but_last(self, token=None):
            while len(self.left) > 1:
                token = self.step(token)
            return token

    class Halving:
        def __init__(self, parts, low=BF16):
            self.parts, self.low, self.left = parts, low, list(bits)
            self.start()

        def start(self):
            b = self.left[0]
            up = (f // b) % 2
            send, self.keep = [], []
            for part in self.parts:
                v = part.reshape((part.shape[0] // 2, 2) + part.shape[1:])
                send.append(lax.dynamic_index_in_dim(v, 1 - up, 1, keepdims=False).astype(self.low))
                self.keep.append(lax.dynamic_index_in_dim(v, up, 1, keepdims=False))
            self.got = swap(jnp.concatenate(send, axis=-1), b, 0)

        def step(self, token=None):
            got = self.got if token is None else gate(self.got, token)
            at, parts = 0, []
            for keep in self.keep:
                parts.append(keep + got[..., at : at + keep.shape[-1]].astype(F32))
                at += keep.shape[-1]
            self.parts = parts
            self.left.pop(0)
            if self.left:
                self.start()
            return list(parts)

        def upto(self, count, token):
            while len(self.left) > count:
                token = self.step(token)
            return token

        def result(self):
            return jnp.concatenate([p[0] for p in self.parts], axis=-1)

    def slots_of(v):
        y = across(v)
        return [v, y, core(v), core(y)]

    n_img, length = tokens.shape[0], tokens.shape[1]
    images = range(n_img)
    quarter = D // nc
    rows_w = D // nf
    wide = 4 * D // nf // nc
    piece = rows_w // nc
    half = 2 * PAD

    mask_rows = jnp.pad(key_mask.astype(BF16), ((0, 0), (0, D - length)))[:, None, :]
    x_own = jnp.concatenate(
        [tokens, mask_rows, jnp.zeros((n_img, PAD - length - 1, D), BF16)], axis=1
    )
    x_slots = slots_of(x_own)

    small = jnp.concatenate(
        [
            norm_gains,
            norm_shifts,
            qv_bias,
            out_bias[None],
            fc2_bias[None],
            fc1_bias.reshape(4, D // nf),
        ],
        axis=0,
    )
    small = jnp.pad(small, ((0, 4), (0, 128 - D // nf)))
    qkv_w = Doubling(pick_qkv(c, qkv_weight, small), rows_w)

    out_pairs = []
    for fs in range(nf):
        for j in range(nc):
            dst_f = (fs % (nf // 4)) * 4 + j
            out_pairs.append((fs * nc + j, dst_f * nc + fs // (nf // 4)))
    out_back = [(b, a) for a, b in out_pairs]
    out_part = lax.dynamic_slice_in_dim(out_weight, c * piece, piece, 0)
    out_part = lax.ppermute(out_part, axes, out_pairs)
    token = qkv_w.step(out_part)
    out_w = Doubling(gate(out_part, token))
    token = qkv_w.all_but_last(token)
    fc1_w = Doubling(gate(pick_fc1(c, fc1_weight, wide), token))
    fc2_part = lax.dynamic_slice_in_dim(fc2_weight, c * wide, wide, 0)

    position = c * length + jnp.arange(length)
    keep = (position < LIVE)[None, :] & (slot_valid[:, None] > 0)
    g_own = jnp.where(keep[:, :, None], out_grad, jnp.zeros((), BF16))
    g_own = jnp.pad(g_own, ((0, 0), (0, PAD - length), (0, 0)))
    g_slots = slots_of(gate(g_own, x_slots[1]))


    token = fc1_w.step([token, x_slots[1]])
    token = out_w.step([token, g_slots[1]])
    token = qkv_w.step(token)
    w_qkv, small = qkv_w.buf, qkv_w.small
    fc1_shift = lax.dynamic_slice_in_dim(small, 8 + c, 1, 0)
    qkv_shift = []
    for p in range(2):
        q_shift = lax.dynamic_slice(small, (4, c * quarter + p * 128), (1, 128))
        v_shift = lax.dynamic_slice(small, (5, c * quarter + p * 128), (1, 128))
        qkv_shift.append(jnp.concatenate([q_shift, jnp.zeros_like(q_shift), v_shift], axis=1))

    def rows_of(v, i, first=0, count=4):
        return v[(4 * i + first) * PAD : (4 * i + first + count) * PAD]

    def send_rows(left, weight, i, product=dot):
        return product(rows_of(left, i, 2, 2), weight).astype(BF16)

    def mine_rows(left, weight, i, got, product=dot):
        return (product(rows_of(left, i, 0, 2), weight) + got.astype(F32)).astype(BF16)

    def total_of(mine, got):
        got = jnp.concatenate([got[PAD:], got[:PAD]], axis=0)
        return (mine.astype(F32) + got.astype(F32)).astype(BF16)

    def core_halves(v):
        return [core(v[:PAD]), core(v[PAD:])]

    normed, bias = prepare([gate(x_slots[0], token)] + x_slots[1:], small)
    qkv, lse, contexts = [], [], []
    token = out_w.all_but_last([token, normed])
    token = fc1_w.all_but_last(token)
    fc2_w = Doubling(gate(fc2_part, token))
    for p in range(2):
        qkv.append((dot(normed, w_qkv[p]) + qkv_shift[p]).astype(BF16))
        out = attention(n_img, gate(qkv[p], token), bias)
        contexts.append(out[0])
        lse.append(out[1])
        token = out[0]
    token = out_w.step(token)
    w_out = flat(out_w.buf)
    token = fc2_w.step(token)
    context = jnp.concatenate(contexts, axis=1)
    sends = [send_rows(gate(context, token), w_out, i) for i in images]
    mine1, got1 = [], []
    for i in images:
        mine1.append(mine_rows(context, w_out, i, core(sends[i])))
        got1.append(across(mine1[i]))
    token = fc2_w.all_but_last(mine1[-1])
    g_all = stack_rows(g_slots)

    parts = []
    for i in images:
        if i == n_img - 1:
            token = fc1_w.step(token)
            w_fc1 = flat(fc1_w.buf)
        got = gate(got1[i], token)
        total = total_of(mine1[i], got)
        parts += [mine1[i], got] + core_halves(total)
        token = total
    middle, normed_mid = middle_rows(x_slots, [gate(parts[0], token)] + parts[1:], small)
    token = fc2_w.step(middle)
    w_fc2 = flat(fc2_w.buf)
    pre = dot(gate(normed_mid, token), w_fc1) + fc1_shift
    sig = jax.nn.sigmoid(1.702 * pre)
    hidden = (pre * sig).astype(BF16)
    p_fc2 = dot_tn(hidden, g_all)
    fc2_g = Halving([p_fc2.reshape(nf, -1, D)])

    d_hidden = dot_nt(g_all, w_fc2)
    d_pre = d_hidden * (sig + 1.702 * pre * sig * (1.0 - sig))
    fc1_sum = jnp.sum(d_pre, axis=0, keepdims=True)
    d_pre_low = d_pre.astype(BF16)
    sends = [send_rows(d_pre_low, w_fc1, i, dot_nt) for i in images]
    mine2, got2 = [], []
    for i in images:
        mine2.append(mine_rows(d_pre_low, w_fc1, i, core(sends[i]), dot_nt))
        got2.append(across(gate(mine2[i], *got2)))
    p_fc1 = dot_tn(gate(normed_mid, mine2[-1]), d_pre_low)
    token = p_fc1

    d_mid_low, d_mid_own, mid_sums, d_context = [], [], [], []
    d_raw = [[None] * n_img for _ in range(2)]
    qv_sum, mine3, got3 = [], [], []

    def back_rows(i, token):
        parts = [d_raw[0][i], gate(d_raw[1][i], token)]
        send = sum(dot_nt(parts[p][half:], w_qkv[p]) for p in range(2)).astype(BF16)
        mine = sum(dot_nt(parts[p][:half], w_qkv[p]) for p in range(2))
        mine = (mine + core(send).astype(F32)).astype(BF16)
        mine3.append(mine)
        got3.append(across(gate(mine[PAD:], *got2, *got3)))
        return mine

    for i in images:
        token = total = total_of(mine2[i], gate(got2[i], token))
        low, own, sums = middle_back(i, middle, total, core_halves(total), g_all, small)
        d_mid_low.append(low)
        d_mid_own.append(own)
        mid_sums.append(sums)
        d_context.append(dot_nt(low, w_out).astype(BF16))
        token = low
        if i == n_img - 1:
            p_out = sum(dot_tn(rows_of(context, k), d_mid_low[k]) for k in images)
            out_g = Halving([p_out.reshape(nf, -1, D)])
        sums = []
        for p in range(2):
            d_raw[p][i], s = attention_back(p, i, qkv[p], gate(d_context[i], token), bias, lse[p])
            token = d_raw[p][i]
            sums.append(s)
        qv_sum.append(sums)
        if i == 0:
            token = fc2_g.step(token)
            fc1_g = Halving([gate(p_fc1, token).reshape(nf, -1, D)])

    p_qkv = [
        sum(dot_tn(rows_of(normed, k), gate(d_raw[p][k], token)) for k in images).reshape(nf, -1, 384)
        for p in range(2)
    ]
    qkv_g = Halving(p_qkv)
    token = back_rows(0, p_qkv)
    token = fc2_g.step(token)
    token = fc1_g.step(token)
    token = back_rows(n_img - 1, token)
    token = qkv_g.step(token)
    token = fc2_g.upto(0, token)
    token = out_g.step(token)

    mines, gots = [], []
    sends = [send_rows(gate(hidden, token), w_fc2, i) for i in images]
    for i in images:
        mines.append(mine_rows(hidden, w_fc2, i, core(sends[i])))
        gots.append(across(gate(mines[i][PAD:], got3[-1])))
    token = fc1_g.step(mines[-1]) if fc1_g.left else mines[-1]
    token = out_g.step(token) if out_g.left else token
    token_gradient, tok_sums = tokens_back(length, gate(x_own, token), d_mid_own, mine3, got3, small)
    token = tok_sums

    mid_sum = sum(mid_sums[1:], mid_sums[0])
    fc1_rows = jnp.where((jnp.arange(4) == c)[:, None], fc1_sum, 0.0)
    here = (jnp.arange(D) // quarter == c)[None]
    qv_rows = [sum(s[p] for s in qv_sum[1:]) + qv_sum[0][p] for p in range(2)]
    qv_rows = jnp.concatenate([s[0:2] for s in qv_rows], axis=1)
    qv_rows = jnp.where(here, jnp.tile(qv_rows, (1, nc)), 0.0)
    packed = jnp.concatenate(
        [tok_sums[0:1], mid_sum[0:1], tok_sums[1:2], mid_sum[1:2], qv_rows, mid_sum[2:4], fc1_rows],
        axis=0,
    )
    vectors = Halving([packed.reshape(12, nf, D // nf).transpose(1, 0, 2)], F32)
    token = out_g.upto(0, token)
    out_part = lax.ppermute(out_g.result().astype(BF16), axes, out_back)
    token = vectors.step(token)
    token = fc1_g.upto(0, token)
    token = qkv_g.upto(1, token)
    token = vectors.upto(1, token)
    rest = [v.result().astype(BF16) for v in (fc2_g, fc1_g)]
    rest = jnp.concatenate(rest + [gate(out_part, token)], axis=0)
    rest_slots = slots_of(rest)
    token = qkv_g.upto(0, token)
    qkv_slots = slots_of(qkv_g.result().astype(BF16))
    vectors.upto(0, token)
    packed = vectors.result()
    packed = packed + across(packed)
    packed = packed + core(packed)

    result = result_rows(length, middle, mines, gots, small)
    qkv_full = place_qkv(c, qkv_slots)
    fc2_full, fc1_full, out_full = place_rest(c, rows_w, wide, piece, rest_slots)

    return (
        result,
        token_gradient,
        packed[0:2],
        packed[2:4],
        qkv_full,
        packed[4:6],
        out_full,
        packed[6],
        fc1_full,
        packed[8:12].reshape(-1),
        fc2_full,
        packed[7],
    )


def solution(mesh):
    in_specs = (
        P("fsdp", "ctx", None),
        P("fsdp", "ctx", None),
        P("fsdp", "ctx"),
        P("fsdp"),
        P(None, "fsdp"),
        P(None, "fsdp"),
        P("fsdp", None),
        P(None, "fsdp"),
        P("fsdp", None),
        P("fsdp"),
        P("fsdp", None),
        P("fsdp"),
        P("fsdp", None),
        P("fsdp"),
    )
    out_specs = (
        P("fsdp", "ctx", None),
        P("fsdp", "ctx", None),
        P(None, "fsdp"),
        P(None, "fsdp"),
        P("fsdp", None),
        P(None, "fsdp"),
        P("fsdp", None),
        P("fsdp"),
        P("fsdp", None),
        P("fsdp"),
        P("fsdp", None),
        P("fsdp"),
    )
    step = functools.partial(body, mesh.shape["fsdp"], mesh.shape["ctx"])
    return jax.shard_map(step, mesh=mesh, in_specs=in_specs, out_specs=out_specs, check_vma=False)
```

```python
import functools

import jax
import jax.numpy as jnp
from jax import lax
from jax.experimental import pallas as pl
from jax.experimental.pallas import tpu as pltpu
from jax.sharding import PartitionSpec as P

D = 1024
HEADS = 16
HEAD_DIM = 64
LIVE = 577
PAD = 160
MASK_ROW = 148
NEG = -1e30
F32 = jnp.float32
BF16 = jnp.bfloat16


def dot(a, b):
    return lax.dot_general(a, b, (((1,), (0,)), ((), ())), preferred_element_type=F32)


def dot_nt(a, b):
    return lax.dot_general(a, b, (((1,), (1,)), ((), ())), preferred_element_type=F32)


def dot_tn(a, b):
    return lax.dot_general(a, b, (((0,), (0,)), ((), ())), preferred_element_type=F32)


def layer_norm(values):
    centred = values - jnp.mean(values, axis=-1, keepdims=True)
    inverse = lax.rsqrt(jnp.mean(centred * centred, axis=-1, keepdims=True) + 1e-05)
    return centred * inverse, inverse


def norm_reverse(grad, normed, inverse):
    first = jnp.mean(grad, axis=-1, keepdims=True)
    second = jnp.mean(grad * normed, axis=-1, keepdims=True)
    return inverse * (grad - first - normed * second)


def attn_fwd_kernel(qkv_ref, bias_ref, o_ref, lse_ref):
    lane = lax.broadcasted_iota(jnp.int32, (1, 128), 1)
    q = qkv_ref[:, 0:128] * 0.125
    k = qkv_ref[:, 128:256]
    v = qkv_ref[:, 256:384]
    bias = bias_ref[:, 0:1]
    outs = []
    lse_ref[2:8, :] = jnp.zeros((6, lse_ref.shape[1]), F32)
    for h in range(2):
        qh = jnp.where((lane // 64) == h, q, jnp.zeros_like(q))
        s = dot_nt(k, qh) + bias
        top = jnp.max(s, axis=0, keepdims=True)
        e = jnp.exp(s - top)
        total = jnp.sum(e, axis=0, keepdims=True)
        p = (e * (1.0 / total)).astype(BF16)
        lse_ref[h : h + 1, :] = top + jnp.log(total)
        outs.append(dot_tn(p, v))
    o_ref[...] = jnp.where(lane < 64, outs[0], outs[1]).astype(BF16)


def attn_bwd_kernel(qkv_ref, g_ref, bias_ref, lse_ref, d_ref, sum_ref, dq_acc, dk_acc, dv_acc):
    lane = lax.broadcasted_iota(jnp.int32, (1, 128), 1)
    dk_acc[...] = jnp.zeros_like(dk_acc)
    dv_acc[...] = jnp.zeros_like(dv_acc)

    def head(h, carry):
        q = qkv_ref[:, 0:128] * 0.125
        k = qkv_ref[:, 128:256]
        v = qkv_ref[:, 256:384]
        g = g_ref[...]
        mine = (lane // 64) == h
        qh = jnp.where(mine, q, jnp.zeros_like(q))
        gh = jnp.where(mine, g, jnp.zeros_like(g))
        s = dot_nt(k, qh) + bias_ref[:, 0:1]
        p = jnp.exp(s - lse_ref[pl.ds(h, 1), :])
        dp = dot_nt(v, gh)
        delta = jnp.sum(p * dp, axis=0, keepdims=True)
        ds = (p * (dp - delta)).astype(BF16)
        dv_acc[...] += dot(p.astype(BF16), gh)
        dk_acc[...] += dot(ds, qh)
        dq_acc[...] = jnp.where(mine, dot_tn(ds, k) * 0.125, dq_acc[...])
        return carry

    lax.fori_loop(0, 2, head, 0)
    dq = dq_acc[...]
    dv = dv_acc[...]
    d_ref[:, 0:128] = dq.astype(BF16)
    d_ref[:, 128:256] = dk_acc[...].astype(BF16)
    d_ref[:, 256:384] = dv.astype(BF16)
    sums = [jnp.sum(x, axis=0, keepdims=True) for x in (dq, dv)]
    sum_ref[...] = jnp.concatenate(sums + [jnp.zeros((6, 128), F32)], axis=0)


def params(mib):
    return pltpu.CompilerParams(vmem_limit_bytes=mib << 20)


def cost(us):
    return pl.CostEstimate(flops=int(us * 1e7), bytes_accessed=1024, transcendentals=0)


def attention(n_img, qkv, bias_col):
    rows = qkv.shape[0] // n_img
    spec = lambda w: pl.BlockSpec((rows, w), lambda i: (i, 0))
    return pl.pallas_call(
        attn_fwd_kernel,
        grid=(n_img,),
        in_specs=[spec(384), spec(128)],
        out_specs=[spec(128), pl.BlockSpec((8, rows), lambda i: (i, 0))],
        out_shape=[
            jax.ShapeDtypeStruct((n_img * rows, 128), BF16),
            jax.ShapeDtypeStruct((n_img * 8, rows), F32),
        ],
        compiler_params=params(12),
        cost_estimate=cost(4.0),
        name="attn_fwd",
    )(qkv, bias_col)


def attention_back(pair, image, qkv, grad, bias_col, lse):
    rows = grad.shape[0]
    full = lambda shape: pl.BlockSpec(shape, lambda i: (0, 0))
    return pl.pallas_call(
        attn_bwd_kernel,
        grid=(1,),
        in_specs=[
            pl.BlockSpec((rows, 384), lambda i: (image, 0)),
            pl.BlockSpec((rows, 128), lambda i: (0, pair)),
            pl.BlockSpec((rows, 128), lambda i: (image, 0)),
            pl.BlockSpec((8, rows), lambda i: (image, 0)),
        ],
        out_specs=[full((rows, 384)), full((8, 128))],
        out_shape=[
            jax.ShapeDtypeStruct((rows, 384), BF16),
            jax.ShapeDtypeStruct((8, 128), F32),
        ],
        scratch_shapes=[pltpu.VMEM((rows, 128), F32)] * 3,
        compiler_params=params(12),
        cost_estimate=cost(3.7),
        name="attn_bwd",
    )(qkv, grad, bias_col, lse)


CHUNK = 32
SLOTS = (0, 2, 1, 3)


def prepare_kernel(n_img, *refs):
    slots, (vec_ref, out_ref, bias_ref) = refs[:4], refs[4:]
    gain, add = vec_ref[0:1, :], vec_ref[2:3, :]
    row = lax.broadcasted_iota(jnp.int32, (PAD, PAD), 0)
    lane = lax.broadcasted_iota(jnp.int32, (PAD, PAD), 1)

    def image(i, carry):
        for j, src in enumerate(slots):
            base = pl.multiple_of(i * 4 * PAD + j * PAD, PAD)
            for lo in range(0, PAD, CHUNK):
                normed, _ = layer_norm(src[i, lo : lo + CHUNK, :].astype(F32))
                out_ref[pl.ds(base + lo, CHUNK), :] = (normed * gain + add).astype(BF16)
            mask = src[i, MASK_ROW : MASK_ROW + 1, 0:PAD].astype(F32)
            hidden = jnp.where(row == lane, (1.0 - mask) * NEG, 0.0)
            hidden = jnp.sum(hidden, axis=1, keepdims=True)
            bias_ref[pl.ds(base, PAD), :] = jnp.broadcast_to(hidden, (PAD, 128))
        return carry

    lax.fori_loop(0, n_img, image, 0)


def prepare(slots, small):
    n_img = slots[0].shape[0]
    rows = n_img * 4 * PAD
    return pl.pallas_call(
        functools.partial(prepare_kernel, n_img),
        out_shape=[
            jax.ShapeDtypeStruct((rows, D), BF16),
            jax.ShapeDtypeStruct((rows, 128), F32),
        ],
        compiler_params=params(9),
        cost_estimate=cost(4.2),
        name="prepare",
    )(*slots, small)


def stack_kernel(n_img, *refs):
    slots, out_ref = refs[:4], refs[4]
    for i in range(n_img):
        for j, src in enumerate(slots):
            base = (4 * i + j) * PAD
            out_ref[base : base + PAD, :] = src[i]


def stack_rows(slots):
    n_img = slots[0].shape[0]
    return pl.pallas_call(
        functools.partial(stack_kernel, n_img),
        out_shape=jax.ShapeDtypeStruct((n_img * 4 * PAD, D), BF16),
        compiler_params=params(7),
        cost_estimate=cost(2.0),
        name="stack_rows",
    )(*slots)


def middle_kernel(n_img, *refs):
    slots, parts = refs[:4], refs[4 : 4 + 4 * n_img]
    vec_ref, mid_ref, out_ref = refs[4 + 4 * n_img :]
    shift, gain, add = vec_ref[6:7, :], vec_ref[1:2, :], vec_ref[3:4, :]
    for i in range(n_img):
        mine, got = parts[4 * i], parts[4 * i + 1]
        rest = parts[4 * i + 2 : 4 * i + 4]
        for j, src in enumerate(slots):
            for lo in range(0, PAD, CHUNK):
                near = slice(lo, lo + CHUNK)
                if j < 2:
                    far = slice((1 - j) * PAD + lo, (1 - j) * PAD + lo + CHUNK)
                    own = slice(j * PAD + lo, j * PAD + lo + CHUNK)
                    part = mine[own, :].astype(F32) + got[far, :].astype(F32)
                    part = part.astype(BF16).astype(F32)
                else:
                    part = rest[j - 2][near, :].astype(F32)
                at = slice((4 * i + j) * PAD + lo, (4 * i + j) * PAD + lo + CHUNK)
                m = src[i, near, :].astype(F32) + shift + part
                mid_ref[at, :] = m
                normed, _ = layer_norm(m)
                out_ref[at, :] = (normed * gain + add).astype(BF16)


def middle_rows(slots, parts, small):
    n_img = slots[0].shape[0]
    rows = n_img * 4 * PAD
    return pl.pallas_call(
        functools.partial(middle_kernel, n_img),
        out_shape=[
            jax.ShapeDtypeStruct((rows, D), F32),
            jax.ShapeDtypeStruct((rows, D), BF16),
        ],
        compiler_params=params(18),
        cost_estimate=cost(5.0),
        name="middle",
    )(*slots, *parts, small)


def middle_back_kernel(mid_ref, a_ref, b0_ref, b1_ref, g_ref, vec_ref, low_ref, own_ref, sum_ref):
    gain = vec_ref[1:2, :]
    sums = [jnp.zeros((1, D), F32)] * 4
    for base in range(0, 4 * PAD, CHUNK):
        at = slice(base, base + CHUNK)
        j, lo = base // PAD, base % PAD
        src, lo = (a_ref, base) if j < 2 else ((b0_ref, b1_ref)[j - 2], lo)
        normed, inverse = layer_norm(mid_ref[at, :])
        t = src[lo : lo + CHUNK, :].astype(F32)
        g = g_ref[at, :].astype(F32)
        d = g + norm_reverse(t * gain, normed, inverse)
        low_ref[at, :] = d.astype(BF16)
        if base < PAD:
            own_ref[at, :] = d
            new = [jnp.sum(v, axis=0, keepdims=True) for v in (t * normed, t, d, g)]
            sums = [c + n for c, n in zip(sums, new)]
    sum_ref[...] = jnp.concatenate(list(sums) + [jnp.zeros((4, D), F32)], axis=0)


def middle_back(image, mid, a, rest, g, small):
    rows = 4 * PAD
    full = lambda shape: pl.BlockSpec(shape, lambda i: (0, 0))
    part = pl.BlockSpec((rows, D), lambda i: (image, 0))
    return pl.pallas_call(
        middle_back_kernel,
        grid=(1,),
        in_specs=[part, full(a.shape), full((PAD, D)), full((PAD, D)), part, full(small.shape)],
        out_specs=[full((rows, D)), full((PAD, D)), full((8, D))],
        out_shape=[
            jax.ShapeDtypeStruct((rows, D), BF16),
            jax.ShapeDtypeStruct((PAD, D), F32),
            jax.ShapeDtypeStruct((8, D), F32),
        ],
        compiler_params=params(12),
        cost_estimate=cost(2.2),
        name="middle_back",
    )(mid, a, *rest, g, small)


def pieces_of(length):
    return [(lo, min(CHUNK, length - lo)) for lo in range(0, length, CHUNK)]


def result_kernel(n_img, *refs):
    mids, mine, got = refs[:n_img], refs[n_img : 2 * n_img], refs[2 * n_img : 3 * n_img]
    vec_ref, out_ref = refs[3 * n_img :]
    shift = vec_ref[7:8, :]
    for i in range(n_img):
        for lo, n in pieces_of(out_ref.shape[1]):
            at = slice(lo, lo + n)
            total = mids[i][at, :] + mine[i][at, :].astype(F32) + got[i][at, :].astype(F32)
            out_ref[i, at, :] = (total + shift).astype(BF16)


def result_rows(length, middle, mine, got, small):
    n_img = len(mine)
    spec = pl.BlockSpec((PAD, D), lambda i: (0, 0))
    own = [pl.BlockSpec((PAD, D), lambda i, k=k: (4 * k, 0)) for k in range(n_img)]
    return pl.pallas_call(
        functools.partial(result_kernel, n_img),
        grid=(1,),
        in_specs=own + [spec] * (2 * n_img) + [pl.BlockSpec(small.shape, lambda i: (0, 0))],
        out_specs=pl.BlockSpec((n_img, length, D), lambda i: (0, 0, 0)),
        out_shape=jax.ShapeDtypeStruct((n_img, length, D), BF16),
        compiler_params=params(7),
        cost_estimate=cost(1.5),
        name="result",
    )(*[middle] * n_img, *mine, *got, small)


def tokens_back_kernel(n_img, x_ref, *refs):
    dmid, mine, got = refs[:n_img], refs[n_img : 2 * n_img], refs[2 * n_img : 3 * n_img]
    vec_ref, out_ref, sum_ref = refs[3 * n_img :]
    gain = vec_ref[0:1, :]
    first = jnp.zeros((1, D), F32)
    second = jnp.zeros((1, D), F32)
    for i in range(n_img):
        for lo, n in pieces_of(out_ref.shape[1]):
            at = slice(lo, lo + n)
            normed, inverse = layer_norm(x_ref[i, at, :].astype(F32))
            u = mine[i][at, :].astype(F32) + got[i][at, :].astype(F32)
            first = first + jnp.sum(u * normed, axis=0, keepdims=True)
            second = second + jnp.sum(u, axis=0, keepdims=True)
            d = dmid[i][at, :] + norm_reverse(u * gain, normed, inverse)
            out_ref[i, at, :] = d.astype(BF16)
    sum_ref[...] = jnp.concatenate([first, second, jnp.zeros((6, D), F32)], axis=0)


def tokens_back(length, x, dmid, mine, got, small):
    n_img = len(dmid)
    spec = pl.BlockSpec((PAD, D), lambda i: (0, 0))
    return pl.pallas_call(
        functools.partial(tokens_back_kernel, n_img),
        grid=(1,),
        in_specs=[pl.BlockSpec(x.shape, lambda i: (0, 0, 0))]
        + [spec] * (3 * n_img)
        + [pl.BlockSpec(small.shape, lambda i: (0, 0))],
        out_specs=[
            pl.BlockSpec((n_img, length, D), lambda i: (0, 0, 0)),
            pl.BlockSpec((8, D), lambda i: (0, 0)),
        ],
        out_shape=[
            jax.ShapeDtypeStruct((n_img, length, D), BF16),
            jax.ShapeDtypeStruct((8, D), F32),
        ],
        compiler_params=params(7),
        cost_estimate=cost(2.0),
        name="tokens_back",
    )(x, *dmid, *mine, *got, small)


def pick_qkv_kernel(c_ref, w_ref, small_ref, out_ref):
    c = c_ref[0]
    rows = w_ref.shape[0]
    for p in range(2):
        for k in range(3):
            at = pl.multiple_of(k * D + c * 256 + p * 128, 128)
            to = p * 384 + k * 128
            out_ref[0:rows, to : to + 128] = w_ref[:, pl.ds(at, 128)]
    extra = small_ref.shape[0]
    out_ref[rows : rows + extra, 0:128] = small_ref[...]
    out_ref[rows : rows + extra, 128:768] = jnp.zeros((extra, 640), BF16)


def pick_qkv(c, weight, small):
    rows = weight.shape[0]
    smem = pl.BlockSpec(memory_space=pltpu.SMEM)
    vmem = pl.BlockSpec(memory_space=pltpu.VMEM)
    return pl.pallas_call(
        pick_qkv_kernel,
        in_specs=[smem, vmem, vmem],
        out_specs=vmem,
        out_shape=jax.ShapeDtypeStruct((rows + small.shape[0], 768), BF16),
        compiler_params=params(4),
        cost_estimate=cost(1.0),
        name="pick_qkv",
    )(c.astype(jnp.int32).reshape(1), weight, small)


def pick_fc1_kernel(wide, c_ref, w_ref, out_ref):
    c = c_ref[0]
    for k in range(out_ref.shape[1] // wide):
        at = pl.multiple_of(k * 4 * wide + c * wide, 128)
        out_ref[:, k * wide : (k + 1) * wide] = w_ref[:, pl.ds(at, wide)]


def pick_fc1(c, weight, wide):
    rows = weight.shape[0]
    if wide % 128:
        blocks = weight.reshape(rows, D // wide, 4, wide)
        return lax.dynamic_index_in_dim(blocks, c, 2, keepdims=False).reshape(rows, D)
    vmem = pl.BlockSpec(memory_space=pltpu.VMEM)
    return pl.pallas_call(
        functools.partial(pick_fc1_kernel, wide),
        in_specs=[pl.BlockSpec(memory_space=pltpu.SMEM), vmem],
        out_specs=vmem,
        out_shape=jax.ShapeDtypeStruct((rows, D), BF16),
        compiler_params=params(4),
        cost_estimate=cost(1.0),
        name="pick_fc1",
    )(c.astype(jnp.int32).reshape(1), weight)


def weave_kernel(bit_ref, a_ref, b_ref, o_ref):
    up = bit_ref[0]
    for i in range(a_ref.shape[0]):
        o_ref[i, up] = a_ref[i]
        o_ref[i, 1 - up] = b_ref[i]


def weave(bit, a, b):
    m, r, w = a.shape
    if r % 8 or w % 128:
        up = bit == 1
        low, high = jnp.where(up, b, a), jnp.where(up, a, b)
        return jnp.stack([low, high], axis=1)
    vmem = pl.BlockSpec(memory_space=pltpu.VMEM)
    out = pl.pallas_call(
        weave_kernel,
        in_specs=[pl.BlockSpec(memory_space=pltpu.SMEM), vmem, vmem],
        out_specs=vmem,
        out_shape=jax.ShapeDtypeStruct((m, 2, r, w), a.dtype),
        compiler_params=params(7),
        cost_estimate=cost(0.5 + m * r * w * 2e-6),
        name="weave",
    )(bit.astype(jnp.int32).reshape(1), a, b)
    return out


def weave_split_kernel(rows, bit_ref, a_ref, b_ref, w0_ref, w1_ref, small_ref):
    up = bit_ref[0]
    for i in range(a_ref.shape[0]):
        for src, which in ((a_ref, up), (b_ref, 1 - up)):
            w0_ref[i, which] = src[i, 0:rows, 0:384]
            w1_ref[i, which] = src[i, 0:rows, 384:768]
            at = pl.multiple_of((2 * i + which) * 128, 128)
            small_ref[:, pl.ds(at, 128)] = src[i, rows:, 0:128].astype(F32)


def weave_split(rows, bit, a, b):
    m, r, w = a.shape
    if 2 * m * 128 != D:
        both = weave(bit, a, b).reshape(2 * m, r, w)
        span = D // (2 * m)
        small = both[:, rows:, :span].transpose(1, 0, 2).reshape(r - rows, D)
        weights = both[:, :rows].reshape(-1, w)
        return [weights[:, :384], weights[:, 384:]], small.astype(F32)
    vmem = pl.BlockSpec(memory_space=pltpu.VMEM)
    w0, w1, small = pl.pallas_call(
        functools.partial(weave_split_kernel, rows),
        in_specs=[pl.BlockSpec(memory_space=pltpu.SMEM), vmem, vmem],
        out_specs=[vmem] * 3,
        out_shape=[jax.ShapeDtypeStruct((m, 2, rows, 384), a.dtype)] * 2
        + [jax.ShapeDtypeStruct((r - rows, D), F32)],
        compiler_params=params(6),
        cost_estimate=cost(1.0),
        name="weave_split",
    )(bit.astype(jnp.int32).reshape(1), a, b)
    return [w0.reshape(-1, 384), w1.reshape(-1, 384)], small


def place_qkv_kernel(c_ref, *refs):
    out_ref = refs[-1]
    c = c_ref[0]
    for slot, ref in enumerate(refs[:-1]):
        for pair in range(2):
            for k in range(3):
                at = pl.multiple_of(k * D + (c ^ SLOTS[slot]) * 256 + pair * 128, 128)
                src = pair * 384 + k * 128
                out_ref[:, pl.ds(at, 128)] = ref[:, src : src + 128].astype(F32)


def place_rest_kernel(r, wide, piece, c_ref, *refs):
    slots, (fc2_ref, fc1_ref, out_ref) = refs[:4], refs[4:]
    c = c_ref[0]
    for slot, ref in enumerate(slots):
        q = c ^ SLOTS[slot]
        fc2_ref[pl.ds(pl.multiple_of(q * wide, 8), wide), :] = ref[0:wide, :].astype(F32)
        for f in range(D // wide):
            at = pl.multiple_of(f * 4 * wide + q * wide, 128)
            fc1_ref[:, pl.ds(at, wide)] = ref[wide : wide + r, f * wide : (f + 1) * wide].astype(F32)
        out_ref[pl.ds(pl.multiple_of(q * piece, 8), piece), :] = ref[wide + r :, :].astype(F32)


def in_order(c, slots):
    own, y, core, both = slots
    odd = c % 2 == 1
    low = [jnp.where(odd, core, own), jnp.where(odd, own, core)]
    high = [jnp.where(odd, both, y), jnp.where(odd, y, both)]
    up = c // 2 == 1
    return jnp.stack(
        [jnp.where(up, b, a) for a, b in zip(low, high)]
        + [jnp.where(up, a, b) for a, b in zip(low, high)]
    )


def place_qkv(c, slots):
    r = slots[0].shape[0]
    smem = pl.BlockSpec(memory_space=pltpu.SMEM)
    vmem = pl.BlockSpec(memory_space=pltpu.VMEM)
    return pl.pallas_call(
        place_qkv_kernel,
        in_specs=[smem] + [vmem] * 4,
        out_specs=vmem,
        out_shape=jax.ShapeDtypeStruct((r, 3 * D), F32),
        compiler_params=params(4),
        cost_estimate=cost(1.5),
        name="place_qkv",
    )(c.astype(jnp.int32).reshape(1), *slots)


def place_rest(c, r, wide, piece, slots):
    if wide % 128 or piece % 8:
        full = in_order(c, slots).astype(F32)
        fc2 = full[:, :wide].reshape(-1, D)
        fc1 = full[:, wide : wide + r].reshape(4, r, D // wide, wide)
        fc1 = fc1.transpose(1, 2, 0, 3).reshape(r, 4 * D)
        return fc2, fc1, full[:, wide + r :].reshape(-1, D)
    smem = pl.BlockSpec(memory_space=pltpu.SMEM)
    vmem = pl.BlockSpec(memory_space=pltpu.VMEM)
    return pl.pallas_call(
        functools.partial(place_rest_kernel, r, wide, piece),
        in_specs=[smem] + [vmem] * 4,
        out_specs=[vmem] * 3,
        out_shape=[
            jax.ShapeDtypeStruct((4 * wide, D), F32),
            jax.ShapeDtypeStruct((r, 4 * D), F32),
            jax.ShapeDtypeStruct((4 * piece, D), F32),
        ],
        compiler_params=params(9),
        cost_estimate=cost(4.0),
        name="place_rest",
    )(c.astype(jnp.int32).reshape(1), *slots)


def gate(value, *after):
    flat = [v for a in after for v in (a if isinstance(a, (list, tuple)) else [a])]
    return lax.optimization_barrier((value, *flat))[0]


def body(
    nf,
    nc,
    tokens,
    out_grad,
    key_mask,
    slot_valid,
    norm_gains,
    norm_shifts,
    qkv_weight,
    qv_bias,
    out_weight,
    out_bias,
    fc1_weight,
    fc1_bias,
    fc2_weight,
    fc2_bias,
):
    f = lax.axis_index("fsdp")
    c = lax.axis_index("ctx")
    axes = ("fsdp", "ctx")
    bits = []
    while (1 << len(bits)) < nf:
        bits.append(1 << len(bits))

    def swap(v, df, dc):
        pairs = [(i * nc + j, (i ^ df) * nc + (j ^ dc)) for i in range(nf) for j in range(nc)]
        return lax.ppermute(v, axes, pairs)

    def core(v):
        return swap(v, 0, 1)

    def across(v):
        return swap(v, 0, 2)

    def flat(buf):
        return buf.reshape((-1,) + buf.shape[2:])

    class Doubling:
        def __init__(self, shard, split=0):
            self.buf, self.left, self.split, self.small = shard[None], list(reversed(bits)), split, None

        def step(self, token=None):
            b = self.left.pop(0)
            other = swap(self.buf, b, 0)
            if token is not None:
                other = gate(other, token)
            bit = (f // b) % 2
            if self.split and not self.left:
                self.buf, self.small = weave_split(self.split, bit, self.buf, other)
                return self.small
            out = weave(bit, self.buf, other)
            self.buf = out.reshape((-1,) + out.shape[2:])
            return out

        def all_but_last(self, token=None):
            while len(self.left) > 1:
                token = self.step(token)
            return token

    class Halving:
        def __init__(self, parts, low=BF16):
            self.parts, self.low, self.left = parts, low, list(bits)
            self.start()

        def start(self):
            b = self.left[0]
            up = (f // b) % 2
            send, self.keep = [], []
            for part in self.parts:
                v = part.reshape((part.shape[0] // 2, 2) + part.shape[1:])
                send.append(lax.dynamic_index_in_dim(v, 1 - up, 1, keepdims=False).astype(self.low))
                self.keep.append(lax.dynamic_index_in_dim(v, up, 1, keepdims=False))
            self.got = swap(jnp.concatenate(send, axis=-1), b, 0)

        def step(self, token=None):
            got = self.got if token is None else gate(self.got, token)
            at, parts = 0, []
            for keep in self.keep:
                parts.append(keep + got[..., at : at + keep.shape[-1]].astype(F32))
                at += keep.shape[-1]
            self.parts = parts
            self.left.pop(0)
            if self.left:
                self.start()
            return list(parts)

        def upto(self, count, token):
            while len(self.left) > count:
                token = self.step(token)
            return token

        def result(self):
            return jnp.concatenate([p[0] for p in self.parts], axis=-1)

    def slots_of(v):
        y = across(v)
        return [v, y, core(v), core(y)]

    n_img, length = tokens.shape[0], tokens.shape[1]
    images = range(n_img)
    quarter = D // nc
    rows_w = D // nf
    wide = 4 * D // nf // nc
    piece = rows_w // nc
    half = 2 * PAD

    mask_rows = jnp.pad(key_mask.astype(BF16), ((0, 0), (0, D - length)))[:, None, :]
    x_own = jnp.concatenate(
        [tokens, mask_rows, jnp.zeros((n_img, PAD - length - 1, D), BF16)], axis=1
    )
    x_slots = slots_of(x_own)

    small = jnp.concatenate(
        [
            norm_gains,
            norm_shifts,
            qv_bias,
            out_bias[None],
            fc2_bias[None],
            fc1_bias.reshape(4, D // nf),
        ],
        axis=0,
    )
    small = jnp.pad(small, ((0, 4), (0, 128 - D // nf)))
    qkv_w = Doubling(pick_qkv(c, qkv_weight, small), rows_w)

    out_pairs = []
    for fs in range(nf):
        for j in range(nc):
            dst_f = (fs % (nf // 4)) * 4 + j
            out_pairs.append((fs * nc + j, dst_f * nc + fs // (nf // 4)))
    out_back = [(b, a) for a, b in out_pairs]
    out_part = lax.dynamic_slice_in_dim(out_weight, c * piece, piece, 0)
    out_part = lax.ppermute(out_part, axes, out_pairs)
    token = qkv_w.step(out_part)
    out_w = Doubling(gate(out_part, token))
    token = qkv_w.all_but_last(token)
    fc1_w = Doubling(gate(pick_fc1(c, fc1_weight, wide), token))
    fc2_part = lax.dynamic_slice_in_dim(fc2_weight, c * wide, wide, 0)

    position = c * length + jnp.arange(length)
    keep = (position < LIVE)[None, :] & (slot_valid[:, None] > 0)
    g_own = jnp.where(keep[:, :, None], out_grad, jnp.zeros((), BF16))
    g_own = jnp.pad(g_own, ((0, 0), (0, PAD - length), (0, 0)))
    g_slots = slots_of(gate(g_own, x_slots[1]))


    token = fc1_w.step([token, x_slots[1]])
    token = out_w.step([token, g_slots[1]])
    token = qkv_w.step(token)
    w_qkv, small = qkv_w.buf, qkv_w.small
    fc1_shift = lax.dynamic_slice_in_dim(small, 8 + c, 1, 0)
    qkv_shift = []
    for p in range(2):
        q_shift = lax.dynamic_slice(small, (4, c * quarter + p * 128), (1, 128))
        v_shift = lax.dynamic_slice(small, (5, c * quarter + p * 128), (1, 128))
        qkv_shift.append(jnp.concatenate([q_shift, jnp.zeros_like(q_shift), v_shift], axis=1))

    def rows_of(v, i, first=0, count=4):
        return v[(4 * i + first) * PAD : (4 * i + first + count) * PAD]

    def send_rows(left, weight, i, product=dot):
        return product(rows_of(left, i, 2, 2), weight).astype(BF16)

    def mine_rows(left, weight, i, got, product=dot):
        return (product(rows_of(left, i, 0, 2), weight) + got.astype(F32)).astype(BF16)

    def total_of(mine, got):
        got = jnp.concatenate([got[PAD:], got[:PAD]], axis=0)
        return (mine.astype(F32) + got.astype(F32)).astype(BF16)

    def core_halves(v):
        return [core(v[:PAD]), core(v[PAD:])]

    normed, bias = prepare([gate(x_slots[0], token)] + x_slots[1:], small)
    qkv, lse, contexts = [], [], []
    token = out_w.all_but_last([token, normed])
    token = fc1_w.all_but_last(token)
    fc2_w = Doubling(gate(fc2_part, token))
    for p in range(2):
        qkv.append((dot(normed, w_qkv[p]) + qkv_shift[p]).astype(BF16))
        out = attention(n_img, gate(qkv[p], token), bias)
        contexts.append(out[0])
        lse.append(out[1])
        token = out[0]
    token = out_w.step(token)
    w_out = flat(out_w.buf)
    token = fc2_w.step(token)
    context = jnp.concatenate(contexts, axis=1)
    sends = [send_rows(gate(context, token), w_out, i) for i in images]
    mine1, got1 = [], []
    for i in images:
        mine1.append(mine_rows(context, w_out, i, core(sends[i])))
        got1.append(across(mine1[i]))
    token = fc2_w.all_but_last(mine1[-1])
    g_all = stack_rows(g_slots)

    parts = []
    for i in images:
        if i == n_img - 1:
            token = fc1_w.step(token)
            w_fc1 = flat(fc1_w.buf)
        got = gate(got1[i], token)
        total = total_of(mine1[i], got)
        parts += [mine1[i], got] + core_halves(total)
        token = total
    middle, normed_mid = middle_rows(x_slots, [gate(parts[0], token)] + parts[1:], small)
    token = fc2_w.step(middle)
    w_fc2 = flat(fc2_w.buf)
    pre = dot(gate(normed_mid, token), w_fc1) + fc1_shift
    sig = jax.nn.sigmoid(1.702 * pre)
    hidden = (pre * sig).astype(BF16)
    p_fc2 = dot_tn(hidden, g_all)
    fc2_g = Halving([p_fc2.reshape(nf, -1, D)])

    d_hidden = dot_nt(g_all, w_fc2)
    d_pre = d_hidden * (sig + 1.702 * pre * sig * (1.0 - sig))
    fc1_sum = jnp.sum(d_pre, axis=0, keepdims=True)
    d_pre_low = d_pre.astype(BF16)
    sends = [send_rows(d_pre_low, w_fc1, i, dot_nt) for i in images]
    mine2, got2 = [], []
    for i in images:
        mine2.append(mine_rows(d_pre_low, w_fc1, i, core(sends[i]), dot_nt))
        got2.append(across(gate(mine2[i], *got2)))
    p_fc1 = dot_tn(gate(normed_mid, mine2[-1]), d_pre_low)
    token = p_fc1

    d_mid_low, d_mid_own, mid_sums, d_context = [], [], [], []
    d_raw = [[None] * n_img for _ in range(2)]
    qv_sum, mine3, got3 = [], [], []

    def back_rows(i, token):
        parts = [d_raw[0][i], gate(d_raw[1][i], token)]
        send = sum(dot_nt(parts[p][half:], w_qkv[p]) for p in range(2)).astype(BF16)
        mine = sum(dot_nt(parts[p][:half], w_qkv[p]) for p in range(2))
        mine = (mine + core(send).astype(F32)).astype(BF16)
        mine3.append(mine)
        got3.append(across(gate(mine[PAD:], *got2, *got3)))
        return mine

    for i in images:
        token = total = total_of(mine2[i], gate(got2[i], token))
        low, own, sums = middle_back(i, middle, total, core_halves(total), g_all, small)
        d_mid_low.append(low)
        d_mid_own.append(own)
        mid_sums.append(sums)
        d_context.append(dot_nt(low, w_out).astype(BF16))
        token = low
        if i == n_img - 1:
            p_out = sum(dot_tn(rows_of(context, k), d_mid_low[k]) for k in images)
            out_g = Halving([p_out.reshape(nf, -1, D)])
        sums = []
        for p in range(2):
            d_raw[p][i], s = attention_back(p, i, qkv[p], gate(d_context[i], token), bias, lse[p])
            token = d_raw[p][i]
            sums.append(s)
        qv_sum.append(sums)
        if i == 0:
            token = fc2_g.step(token)
            fc1_g = Halving([gate(p_fc1, token).reshape(nf, -1, D)])

    p_qkv = [
        sum(dot_tn(rows_of(normed, k), gate(d_raw[p][k], token)) for k in images).reshape(nf, -1, 384)
        for p in range(2)
    ]
    qkv_g = Halving(p_qkv)
    token = back_rows(0, p_qkv)
    token = fc2_g.step(token)
    token = fc1_g.step(token)
    token = back_rows(n_img - 1, token)
    token = qkv_g.step(token)
    token = fc2_g.upto(0, token)
    token = out_g.step(token)

    mines, gots = [], []
    sends = [send_rows(gate(hidden, token), w_fc2, i) for i in images]
    for i in images:
        mines.append(mine_rows(hidden, w_fc2, i, core(sends[i])))
        gots.append(across(gate(mines[i][PAD:], got3[-1])))
    token = fc1_g.step(mines[-1]) if fc1_g.left else mines[-1]
    token = out_g.step(token) if out_g.left else token
    token_gradient, tok_sums = tokens_back(length, gate(x_own, token), d_mid_own, mine3, got3, small)
    token = tok_sums

    mid_sum = sum(mid_sums[1:], mid_sums[0])
    fc1_rows = jnp.where((jnp.arange(4) == c)[:, None], fc1_sum, 0.0)
    here = (jnp.arange(D) // quarter == c)[None]
    qv_rows = [sum(s[p] for s in qv_sum[1:]) + qv_sum[0][p] for p in range(2)]
    qv_rows = jnp.concatenate([s[0:2] for s in qv_rows], axis=1)
    qv_rows = jnp.where(here, jnp.tile(qv_rows, (1, nc)), 0.0)
    packed = jnp.concatenate(
        [tok_sums[0:1], mid_sum[0:1], tok_sums[1:2], mid_sum[1:2], qv_rows, mid_sum[2:4], fc1_rows],
        axis=0,
    )
    vectors = Halving([packed.reshape(12, nf, D // nf).transpose(1, 0, 2)], F32)
    token = out_g.upto(0, token)
    out_part = lax.ppermute(out_g.result().astype(BF16), axes, out_back)
    token = vectors.step(token)
    token = fc1_g.upto(0, token)
    token = qkv_g.upto(1, token)
    token = vectors.upto(1, token)
    rest = [v.result().astype(BF16) for v in (fc2_g, fc1_g)]
    rest = jnp.concatenate(rest + [gate(out_part, token)], axis=0)
    rest_slots = slots_of(rest)
    token = qkv_g.upto(0, token)
    qkv_slots = slots_of(qkv_g.result().astype(BF16))
    vectors.upto(0, token)
    packed = vectors.result()
    packed = packed + across(packed)
    packed = packed + core(packed)

    result = result_rows(length, middle, mines, gots, small)
    qkv_full = place_qkv(c, qkv_slots)
    fc2_full, fc1_full, out_full = place_rest(c, rows_w, wide, piece, rest_slots)

    return (
        result,
        token_gradient,
        packed[0:2],
        packed[2:4],
        qkv_full,
        packed[4:6],
        out_full,
        packed[6],
        fc1_full,
        packed[8:12].reshape(-1),
        fc2_full,
        packed[7],
    )


def solution(mesh):
    in_specs = (
        P("fsdp", "ctx", None),
        P("fsdp", "ctx", None),
        P("fsdp", "ctx"),
        P("fsdp"),
        P(None, "fsdp"),
        P(None, "fsdp"),
        P("fsdp", None),
        P(None, "fsdp"),
        P("fsdp", None),
        P("fsdp"),
        P("fsdp", None),
        P("fsdp"),
        P("fsdp", None),
        P("fsdp"),
    )
    out_specs = (
        P("fsdp", "ctx", None),
        P("fsdp", "ctx", None),
        P(None, "fsdp"),
        P(None, "fsdp"),
        P("fsdp", None),
        P(None, "fsdp"),
        P("fsdp", None),
        P("fsdp"),
        P("fsdp", None),
        P("fsdp"),
        P("fsdp", None),
        P("fsdp"),
    )
    step = functools.partial(body, mesh.shape["fsdp"], mesh.shape["ctx"])
    return jax.shard_map(step, mesh=mesh, in_specs=in_specs, out_specs=out_specs, check_vma=False)
```
